256 devices in a mesh: mem: 16 (over z, y_lo), col: 16 (over y_hi, x, core).
Axes of the slice: x: 4, y: 4 (y_hi: 2, y_lo: 2; y = y_hi * 2 + y_lo), z: 8, core: 2. Of those that a mesh axis runs over, the one named last changes fastest.
Arguments:
- perturbations: bfloat16 [256, 262144], P('mem', 'col'), may hold values from -6 to 6
- obs_index: int32 [4, 256], replicated, may hold values from 0 to 262143, as said below
- obs_var: float32 [4, 256], replicated, may hold values from 1 to 8
Outputs:
- analysis: bfloat16 [256, 262144], P('mem', 'col')
The draws below stay inside these ranges and needn't reach their ends.
Inputs may be any that keep to these rules, and one draw needn't show every extreme that they name: `obs_index`: within each batch, every aligned block of 1024 consecutive state indices holds exactly 1 of the batch's observations, all at different indices; their order within the batch is arbitrary.
All inputs are finite; a program needn't handle non-finite values.
Results may differ from the reference program's by a relative error of at most 0.0075.
Values may be sent and summed in bfloat16 or wider, within the bound.
No kernel may reach another device: no remote copies, remote signals or barrier semaphores. Data moves between devices by JAX's collectives and lax.ppermute only.
A program may use at most 64 MiB of HBM per device.

```python
import math
import jax
import jax.numpy as jnp
from jax import lax

MEMBERS = 256
C_DEV = 1024
OB_DEV = 1
NB = 4
NOB = 256
STATE = 262144


def draw_obs_index(key, part):
    blocks_count = STATE // C_DEV
    slot_span = C_DEV // OB_DEV
    batches_list = []
    for which_batch in range(NB):
        batch_key = jax.random.fold_in(key, which_batch)
        offsets = jax.random.randint(jax.random.fold_in(batch_key, 1), (blocks_count, OB_DEV), 0, slot_span)
        base_index = jnp.arange(blocks_count, dtype=jnp.int32)[:, None] * C_DEV + jnp.arange(OB_DEV, dtype=jnp.int32)[None, :] * slot_span
        flat_index = (base_index + offsets).reshape(-1)
        order = jax.random.permutation(jax.random.fold_in(batch_key, 2), blocks_count * OB_DEV)
        batches_list.append(flat_index[order])
    return jnp.stack(batches_list, axis=0).astype(jnp.int32)


def block_scale(stream_key, dims, split, low, top_value):
    def one(dim, parts):
        heights = jax.random.uniform(jax.random.fold_in(jax.random.fold_in(stream_key, 6), dim), (parts,), jnp.float32, low / len(split), top_value / len(split))
        return jnp.repeat(jnp.exp(heights), dims[dim] // parts).reshape((-1,) + (1,) * (len(dims) - dim - 1))

    level = one(*split[0])
    for cut in split[1:]:
        level = level * one(*cut)
    return level


def bell_draw(own_key, shape, width, most, shards=(), held_as=jnp.bfloat16):
    array = width * jax.random.normal(own_key, shape, jnp.float32)
    if shards:
        array = array * block_scale(own_key, shape, shards, -0.22, 0.18)
    return jnp.clip(array, -most, most).astype(held_as)


def setup_inputs(seed: int = 0) -> dict:
    keys = jax.random.split(jax.random.key(seed), 4)
    return {
        "perturbations": bell_draw(keys[0], (MEMBERS, STATE), 1.0, 6.0, ((0, 16), (1, 16))),
        "obs_index": draw_obs_index(jax.random.fold_in(keys[3], 71), 0),
        "obs_var": jnp.clip(jnp.exp(jax.random.uniform(keys[2], (NB, NOB), jnp.float32, math.log(1.0), math.log(8.0))), 1.0, 8.0),
    }


def transform_matrix(observed, variance, members):
    inverse_count = 1.0 / (members - 1)
    innov_cov = jnp.dot(observed.T.astype(jnp.float32), observed.astype(jnp.float32), preferred_element_type=jnp.float32) * inverse_count + jnp.diag(variance)
    factor = jnp.linalg.cholesky(innov_cov)
    first_solve = jax.scipy.linalg.solve_triangular(factor, observed.T.astype(jnp.float32), lower=True)
    shifted = factor + jnp.diag(jnp.sqrt(variance))
    second = jax.scipy.linalg.solve_triangular(shifted, first_solve, trans=1, lower=True)
    product = jnp.dot(observed.astype(jnp.float32), second, precision=lax.Precision.HIGHEST)
    identity = jnp.eye(members, dtype=jnp.float32)
    return (identity - product * inverse_count).astype(jnp.bfloat16)

def reference(perturbations, obs_index, obs_var):
    ensemble = perturbations
    for which_batch in range(NB):
        observed = jnp.take(ensemble, obs_index[which_batch], axis=1)
        weights = transform_matrix(observed, obs_var[which_batch], MEMBERS)
        ensemble = jnp.dot(weights.astype(jnp.float32), ensemble.astype(jnp.float32), preferred_element_type=jnp.float32).astype(jnp.bfloat16)
    return ensemble
```

```python
import jax
import jax.numpy as jnp
from jax import lax
from jax.experimental import pallas as pl
from jax.experimental.pallas import tpu as pltpu
from jax.sharding import PartitionSpec as P

F32 = jnp.float32
BF16 = jnp.bfloat16
STEPS = 4
RESIDUAL_MAX = 4e-3
PAD = 128


def mul(a, b):
    return lax.dot_general(
        a.astype(BF16), b.astype(BF16), (((1,), (0,)), ((), ())), preferred_element_type=F32
    )


def mul_t(a, b):
    return lax.dot_general(
        a.astype(BF16), b.astype(BF16), (((1,), (1,)), ((), ())), preferred_element_type=F32
    )


def iotas(n):
    rows = lax.broadcasted_iota(jnp.int32, (n, n), 0)
    cols = lax.broadcasted_iota(jnp.int32, (n, n), 1)
    return rows, cols


def fast_transform(obs, obs_t, var_row, var_col, inverse_count):
    n = obs.shape[1]
    rows, cols = iotas(n)
    wide = obs.astype(F32)
    wide_t = obs_t.astype(F32)
    dr = lax.rsqrt(jnp.sum(wide * wide, axis=0, keepdims=True) * inverse_count + var_row)
    dc = lax.rsqrt(jnp.sum(wide_t * wide_t, axis=1, keepdims=True) * inverse_count + var_col)
    gram = mul_t(obs_t, obs_t)
    error = jnp.where(rows == cols, 0.0, gram * (dc * inverse_count) * dr)
    lower = jnp.where(rows > cols, 1.0, jnp.where(rows == cols, 0.5, 0.0))
    first_t = wide * (dr * (inverse_count**0.5))
    factor = None
    for step in range(STEPS):
        f = error * lower
        half = f.astype(BF16)
        if step == 0:
            factor = jnp.where(rows == cols, 1.0, 0.0) - f
        else:
            factor = factor - mul(half, factor)
        first_t = first_t - mul_t(first_t, half)
        if step < STEPS - 1:
            y = (error - f) - mul(half, error)
            error = y - (error - f) - mul_t(y, half)
    left = jnp.sum(error * error)
    x = jnp.sqrt(var_row) * dr
    diagonal = jnp.sum(jnp.where(rows == cols, factor, 0.0), axis=0, keepdims=True) * x
    scale = 1.0 / (1.0 + diagonal)
    b = jnp.where(rows > cols, factor * (x * scale), 0.0)
    b2 = mul(b, b)
    second_t = first_t * scale
    second_t = second_t - mul(second_t, b)
    b4 = mul(b2, b2)
    second_t = second_t + mul(second_t, b2)
    second_t = second_t + mul(second_t, b4)
    left = jnp.maximum(left, jnp.sum(b4 * b4))
    product = mul_t(first_t, second_t)
    transform = jnp.where(rows == cols, 1.0, 0.0) - product
    return transform.astype(BF16), left


def exact(a, b, dims):
    return lax.dot_general(
        a, b, (dims, ((), ())), precision=lax.Precision.HIGHEST, preferred_element_type=F32
    )


def slow_transform(obs, obs_t, var_row, cov_ref, inv_ref, shift_ref, inverse_count):
    n = obs.shape[1]
    rows, cols = iotas(n)
    on_diagonal = rows == cols
    gram = mul_t(obs_t, obs_t) * inverse_count
    cov_ref[...] = gram + jnp.where(on_diagonal, var_row, 0.0)
    inv_ref[...] = jnp.where(on_diagonal, 1.0, 0.0)
    shift_ref[...] = jnp.where(on_diagonal, 1.0, 0.0)
    lane = lax.broadcasted_iota(jnp.int32, (1, n), 1)
    sublane = lax.broadcasted_iota(jnp.int32, (n, 1), 0)

    def eliminate(j, carry):
        cov = cov_ref[...]
        cov_row = cov_ref[pl.ds(j, 1), :]
        column = jnp.sum(jnp.where(cols == j, cov, 0.0), axis=1, keepdims=True)
        pivot = jnp.sum(jnp.where(lane == j, cov_row, 0.0), axis=1, keepdims=True)
        noise = jnp.sum(jnp.where(lane == j, var_row, 0.0), axis=1, keepdims=True)
        root = jnp.sqrt(pivot)
        below = jnp.where(sublane > j, column / root, 0.0)
        inv_row = inv_ref[pl.ds(j, 1), :] / root
        shift_row = shift_ref[pl.ds(j, 1), :] / (root + jnp.sqrt(noise))
        cov_ref[...] = cov - below * (cov_row / root)
        inv_ref[...] = jnp.where(sublane == j, inv_row, inv_ref[...] - below * inv_row)
        shift_ref[...] = jnp.where(sublane == j, shift_row, shift_ref[...] - below * shift_row)
        return carry

    lax.fori_loop(0, n, eliminate, 0)
    first_t = exact(obs.astype(F32), inv_ref[...], ((1,), (1,)))
    second_t = exact(first_t, shift_ref[...], ((1,), (0,)))
    product = exact(obs.astype(F32), second_t, ((1,), (1,)))
    transform = jnp.where(on_diagonal, 1.0, 0.0) - product * inverse_count
    return transform.astype(BF16)


def transform_kernel(
    seen_ref, index_ref, var_ref, var_col_ref, weights_ref,
    obs_ref, obs_t_ref, cov_ref, inv_ref, shift_ref, *, block_cols, inverse_count
):
    batches, observations = var_ref.shape
    per_batch = seen_ref.shape[1] // batches
    rows, cols = iotas(observations)
    eye = jnp.where(rows == cols, 1.0, 0.0).astype(BF16)

    def load():
        for batch in range(batches):
            place = index_ref[:, batch : batch + 1] // block_cols
            order = jnp.where(cols == place, 1.0, 0.0)
            seen = seen_ref[:, batch * per_batch : (batch + 1) * per_batch, :]
            obs_t = mul(order, seen.reshape(observations, seen.shape[2])).astype(BF16)
            obs_t_ref[batch] = obs_t
            obs_ref[batch] = mul_t(eye, obs_t).astype(BF16)

    def advance(weights, batch):
        weights_ref[batch] = weights
        for later in range(batch + 1, batches):
            obs = obs_ref[later]
            obs_t = obs_t_ref[later]
            obs_ref[later] = mul(weights, obs).astype(BF16)
            obs_t_ref[later] = mul_t(obs_t, weights).astype(BF16)

    load()
    left = jnp.float32(0.0)
    for batch in range(batches):
        weights, part = fast_transform(
            obs_ref[batch], obs_t_ref[batch], var_ref[batch : batch + 1, :],
            var_col_ref[:, batch : batch + 1], inverse_count,
        )
        left = jnp.maximum(left, part)
        advance(weights, batch)

    @pl.when(jnp.logical_not(left <= RESIDUAL_MAX))
    def _():
        load()
        for batch in range(batches):
            weights = slow_transform(
                obs_ref[batch], obs_t_ref[batch], var_ref[batch : batch + 1, :],
                cov_ref, inv_ref, shift_ref, inverse_count,
            )
            advance(weights, batch)


def transforms(seen, index, var, members, block_cols):
    batches, observations = var.shape
    square = (observations, observations)
    return pl.pallas_call(
        lambda *refs: transform_kernel(
            *refs, block_cols=block_cols, inverse_count=1.0 / (members - 1)
        ),
        out_shape=jax.ShapeDtypeStruct((batches, members, members), BF16),
        in_specs=[pl.BlockSpec(memory_space=pltpu.VMEM)] * 4,
        out_specs=pl.BlockSpec(memory_space=pltpu.VMEM),
        scratch_shapes=[
            pltpu.VMEM((batches, members, observations), BF16),
            pltpu.VMEM((batches, observations, members), BF16),
            pltpu.VMEM(square, F32),
            pltpu.VMEM(square, F32),
            pltpu.VMEM(square, F32),
        ],
        compiler_params=pltpu.CompilerParams(vmem_limit_bytes=32 << 20),
        cost_estimate=pl.CostEstimate(flops=8 * 10**9, bytes_accessed=1 << 20, transcendentals=0),
        name="transforms",
    )(seen, index.T, var, var.T)


def apply_kernel(weights_ref, block_ref, out_ref):
    batches = weights_ref.shape[0]
    columns = out_ref.shape[1]
    chunk = min(columns, 512)
    for start in range(0, columns, chunk):
        piece = slice(start, start + chunk)
        part = block_ref[:, piece]
        for batch in range(batches):
            part = mul(weights_ref[batch], part).astype(BF16)
        out_ref[:, piece] = part


def apply(weights, block):
    return pl.pallas_call(
        apply_kernel,
        out_shape=jax.ShapeDtypeStruct(block.shape, BF16),
        in_specs=[pl.BlockSpec(memory_space=pltpu.VMEM)] * 2,
        out_specs=pl.BlockSpec(memory_space=pltpu.VMEM),
        compiler_params=pltpu.CompilerParams(vmem_limit_bytes=16 << 20),
        name="apply",
    )(weights, block)


def select_kernel(first_ref, block_ref, index_ref, seen_ref, *, block_cols):
    batches = index_ref.shape[0]
    members, group_cols = block_ref.shape
    blocks = group_cols // block_cols
    local = index_ref[...] - first_ref[0]
    lane = lax.broadcasted_iota(jnp.int32, (1, block_cols), 1)
    slot = lax.broadcasted_iota(jnp.int32, (1, PAD), 1)
    seen = jnp.zeros((members, PAD), F32)
    for block in range(blocks):
        inside = local - block * block_cols
        inside = jnp.where((inside >= 0) & (inside < block_cols), inside, 0).astype(F32)
        offsets = jnp.sum(inside, axis=1, keepdims=True).astype(jnp.int32)
        values = block_ref[:, block * block_cols : (block + 1) * block_cols].astype(F32)
        for batch in range(batches):
            chosen = jnp.where(lane == offsets[batch : batch + 1, :], values, 0.0)
            column = jnp.sum(chosen, axis=1, keepdims=True)
            seen = jnp.where(slot == batch * blocks + block, column, seen)
    seen = seen.astype(BF16)
    for peer in range(seen_ref.shape[0]):
        seen_ref[peer] = seen


def select(perturbations, index, first, block_cols, peers):
    members = perturbations.shape[0]
    return pl.pallas_call(
        lambda *refs: select_kernel(*refs, block_cols=block_cols),
        out_shape=jax.ShapeDtypeStruct((peers, members, PAD), BF16),
        in_specs=[pl.BlockSpec(memory_space=pltpu.SMEM)]
        + [pl.BlockSpec(memory_space=pltpu.VMEM)] * 2,
        out_specs=pl.BlockSpec(memory_space=pltpu.VMEM),
        compiler_params=pltpu.CompilerParams(vmem_limit_bytes=16 << 20),
        name="select",
    )(first.reshape(1), perturbations, index)


def on_device(perturbations, obs_index, obs_var):
    members_here, group_cols = perturbations.shape
    mem_count = lax.axis_size("mem")
    col_count = lax.axis_size("col")
    members = members_here * mem_count
    block_cols = group_cols // mem_count
    batches = obs_index.shape[0]
    owned = batches * mem_count
    first = lax.axis_index("col").astype(jnp.int32) * group_cols
    sent = select(perturbations, obs_index, first, block_cols, mem_count)
    seen_group = lax.all_to_all(sent, "mem", split_axis=0, concat_axis=0, tiled=True)
    arranged = perturbations.reshape(members_here, mem_count, block_cols).transpose(1, 0, 2)
    arranged, seen_group = lax.optimization_barrier((arranged, seen_group))
    block = lax.all_to_all(arranged, "mem", split_axis=0, concat_axis=0, tiled=True)
    block = block.reshape(members, block_cols)
    seen_group = seen_group.reshape(members, PAD)[:, :owned].T
    seen = lax.all_to_all(
        jnp.broadcast_to(seen_group, (col_count, owned, members)),
        "col", split_axis=0, concat_axis=0, tiled=True,
    )
    weights = transforms(seen, obs_index, obs_var, members, block_cols)
    ensemble = apply(weights, block)
    returned = lax.all_to_all(
        ensemble.reshape(mem_count, members_here, block_cols), "mem",
        split_axis=0, concat_axis=0, tiled=True,
    )
    return returned.transpose(1, 0, 2).reshape(members_here, group_cols)


def solution(mesh):
    return jax.shard_map(
        on_device,
        mesh=mesh,
        in_specs=(P("mem", "col"), P(), P()),
        out_specs=P("mem", "col"),
        check_vma=False,
    )
```

```python
import jax
import jax.numpy as jnp
from jax import lax
from jax.experimental import pallas as pl
from jax.experimental.pallas import tpu as pltpu
from jax.sharding import PartitionSpec as P

F32 = jnp.float32
BF16 = jnp.bfloat16
STEPS = 4
RESIDUAL_MAX = 4e-3
PAD = 128


def mul(a, b):
    return lax.dot_general(
        a.astype(BF16), b.astype(BF16), (((1,), (0,)), ((), ())), preferred_element_type=F32
    )


def mul_t(a, b):
    return lax.dot_general(
        a.astype(BF16), b.astype(BF16), (((1,), (1,)), ((), ())), preferred_element_type=F32
    )


def iotas(n):
    rows = lax.broadcasted_iota(jnp.int32, (n, n), 0)
    cols = lax.broadcasted_iota(jnp.int32, (n, n), 1)
    return rows, cols


def fast_transform(obs, obs_t, var_row, var_col, inverse_count):
    n = obs.shape[1]
    rows, cols = iotas(n)
    wide = obs.astype(F32)
    wide_t = obs_t.astype(F32)
    dr = lax.rsqrt(jnp.sum(wide * wide, axis=0, keepdims=True) * inverse_count + var_row)
    dc = lax.rsqrt(jnp.sum(wide_t * wide_t, axis=1, keepdims=True) * inverse_count + var_col)
    gram = mul_t(obs_t, obs_t)
    error = jnp.where(rows == cols, 0.0, gram * (dc * inverse_count) * dr)
    lower = jnp.where(rows > cols, 1.0, jnp.where(rows == cols, 0.5, 0.0))
    first_t = wide * (dr * (inverse_count**0.5))
    factor = None
    for step in range(STEPS):
        f = error * lower
        half = f.astype(BF16)
        if step == 0:
            factor = jnp.where(rows == cols, 1.0, 0.0) - f
        else:
            factor = factor - mul(half, factor)
        first_t = first_t - mul_t(first_t, half)
        if step < STEPS - 1:
            y = (error - f) - mul(half, error)
            error = y - (error - f) - mul_t(y, half)
    left = jnp.sum(error * error)
    x = jnp.sqrt(var_row) * dr
    diagonal = jnp.sum(jnp.where(rows == cols, factor, 0.0), axis=0, keepdims=True) * x
    scale = 1.0 / (1.0 + diagonal)
    b = jnp.where(rows > cols, factor * (x * scale), 0.0)
    b2 = mul(b, b)
    second_t = first_t * scale
    second_t = second_t - mul(second_t, b)
    b4 = mul(b2, b2)
    second_t = second_t + mul(second_t, b2)
    second_t = second_t + mul(second_t, b4)
    left = jnp.maximum(left, jnp.sum(b4 * b4))
    product = mul_t(first_t, second_t)
    transform = jnp.where(rows == cols, 1.0, 0.0) - product
    return transform.astype(BF16), left


def exact(a, b, dims):
    return lax.dot_general(
        a, b, (dims, ((), ())), precision=lax.Precision.HIGHEST, preferred_element_type=F32
    )


def slow_transform(obs, obs_t, var_row, cov_ref, inv_ref, shift_ref, inverse_count):
    n = obs.shape[1]
    rows, cols = iotas(n)
    on_diagonal = rows == cols
    gram = mul_t(obs_t, obs_t) * inverse_count
    cov_ref[...] = gram + jnp.where(on_diagonal, var_row, 0.0)
    inv_ref[...] = jnp.where(on_diagonal, 1.0, 0.0)
    shift_ref[...] = jnp.where(on_diagonal, 1.0, 0.0)
    lane = lax.broadcasted_iota(jnp.int32, (1, n), 1)
    sublane = lax.broadcasted_iota(jnp.int32, (n, 1), 0)

    def eliminate(j, carry):
        cov = cov_ref[...]
        cov_row = cov_ref[pl.ds(j, 1), :]
        column = jnp.sum(jnp.where(cols == j, cov, 0.0), axis=1, keepdims=True)
        pivot = jnp.sum(jnp.where(lane == j, cov_row, 0.0), axis=1, keepdims=True)
        noise = jnp.sum(jnp.where(lane == j, var_row, 0.0), axis=1, keepdims=True)
        root = jnp.sqrt(pivot)
        below = jnp.where(sublane > j, column / root, 0.0)
        inv_row = inv_ref[pl.ds(j, 1), :] / root
        shift_row = shift_ref[pl.ds(j, 1), :] / (root + jnp.sqrt(noise))
        cov_ref[...] = cov - below * (cov_row / root)
        inv_ref[...] = jnp.where(sublane == j, inv_row, inv_ref[...] - below * inv_row)
        shift_ref[...] = jnp.where(sublane == j, shift_row, shift_ref[...] - below * shift_row)
        return carry

    lax.fori_loop(0, n, eliminate, 0)
    first_t = exact(obs.astype(F32), inv_ref[...], ((1,), (1,)))
    second_t = exact(first_t, shift_ref[...], ((1,), (0,)))
    product = exact(obs.astype(F32), second_t, ((1,), (1,)))
    transform = jnp.where(on_diagonal, 1.0, 0.0) - product * inverse_count
    return transform.astype(BF16)


def transform_kernel(
    near_ref, far_ref, place_ref, var_ref, var_col_ref, weights_ref,
    obs_ref, obs_t_ref, cov_ref, inv_ref, shift_ref, *, inverse_count
):
    batches, observations = var_ref.shape
    pieces, rows_held, members = near_ref.shape
    per_batch = rows_held // batches
    half = pieces * per_batch
    rows, cols = iotas(observations)
    eye = jnp.where(rows == cols, 1.0, 0.0).astype(BF16)

    def load():
        for batch in range(batches):
            order = jnp.where(cols == place_ref[:, batch : batch + 1], 1.0, 0.0)
            held = slice(batch * per_batch, (batch + 1) * per_batch)
            near = near_ref[:, held, :].reshape(half, members)
            far = far_ref[:, held, :].reshape(half, members)
            obs_t = mul(order, jnp.concatenate([near, far])).astype(BF16)
            obs_t_ref[batch] = obs_t
            obs_ref[batch] = mul_t(eye, obs_t).astype(BF16)

    def advance(weights, batch):
        weights_ref[batch] = weights
        for later in range(batch + 1, batches):
            obs = obs_ref[later]
            obs_t = obs_t_ref[later]
            obs_ref[later] = mul(weights, obs).astype(BF16)
            obs_t_ref[later] = mul_t(obs_t, weights).astype(BF16)

    load()
    left = jnp.float32(0.0)
    for batch in range(batches):
        weights, part = fast_transform(
            obs_ref[batch], obs_t_ref[batch], var_ref[batch : batch + 1, :],
            var_col_ref[:, batch : batch + 1], inverse_count,
        )
        left = jnp.maximum(left, part)
        advance(weights, batch)

    @pl.when(jnp.logical_not(left <= RESIDUAL_MAX))
    def _():
        load()
        for batch in range(batches):
            weights = slow_transform(
                obs_ref[batch], obs_t_ref[batch], var_ref[batch : batch + 1, :],
                cov_ref, inv_ref, shift_ref, inverse_count,
            )
            advance(weights, batch)


def transforms(near, far, place, var, members):
    batches, observations = var.shape
    square = (observations, observations)
    return pl.pallas_call(
        lambda *refs: transform_kernel(
            *refs, inverse_count=1.0 / (members - 1)
        ),
        out_shape=jax.ShapeDtypeStruct((batches, members, members), BF16),
        in_specs=[pl.BlockSpec(memory_space=pltpu.VMEM)] * 5,
        out_specs=pl.BlockSpec(memory_space=pltpu.VMEM),
        scratch_shapes=[
            pltpu.VMEM((batches, members, observations), BF16),
            pltpu.VMEM((batches, observations, members), BF16),
            pltpu.VMEM(square, F32),
            pltpu.VMEM(square, F32),
            pltpu.VMEM(square, F32),
        ],
        compiler_params=pltpu.CompilerParams(vmem_limit_bytes=32 << 20),
        cost_estimate=pl.CostEstimate(flops=8 * 10**9, bytes_accessed=1 << 20, transcendentals=0),
        name="transforms",
    )(near, far, place.T, var, var.T)


def apply_kernel(weights_ref, block_ref, out_ref):
    batches = weights_ref.shape[0]
    columns = out_ref.shape[1]
    chunk = min(columns, 512)
    for start in range(0, columns, chunk):
        piece = slice(start, start + chunk)
        part = block_ref[:, piece]
        for batch in range(batches):
            part = mul(weights_ref[batch], part).astype(BF16)
        out_ref[:, piece] = part


def apply(weights, block):
    return pl.pallas_call(
        apply_kernel,
        out_shape=jax.ShapeDtypeStruct(block.shape, BF16),
        in_specs=[pl.BlockSpec(memory_space=pltpu.VMEM)] * 2,
        out_specs=pl.BlockSpec(memory_space=pltpu.VMEM),
        compiler_params=pltpu.CompilerParams(vmem_limit_bytes=16 << 20),
        name="apply",
    )(weights, block)


def select_kernel(first_ref, block_ref, index_ref, seen_ref, *, block_cols):
    batches = index_ref.shape[0]
    members, group_cols = block_ref.shape
    blocks = group_cols // block_cols
    local = index_ref[...] - first_ref[0]
    lane = lax.broadcasted_iota(jnp.int32, (1, block_cols), 1)
    slot = lax.broadcasted_iota(jnp.int32, (1, PAD), 1)
    seen = jnp.zeros((members, PAD), F32)
    for block in range(blocks):
        inside = local - block * block_cols
        inside = jnp.where((inside >= 0) & (inside < block_cols), inside, 0).astype(F32)
        offsets = jnp.sum(inside, axis=1, keepdims=True).astype(jnp.int32)
        values = block_ref[:, block * block_cols : (block + 1) * block_cols].astype(F32)
        for batch in range(batches):
            chosen = jnp.where(lane == offsets[batch : batch + 1, :], values, 0.0)
            column = jnp.sum(chosen, axis=1, keepdims=True)
            seen = jnp.where(slot == batch * blocks + block, column, seen)
    seen = seen.astype(BF16)
    for peer in range(seen_ref.shape[0]):
        seen_ref[peer] = seen


def select(perturbations, index, first, block_cols, peers):
    members = perturbations.shape[0]
    return pl.pallas_call(
        lambda *refs: select_kernel(*refs, block_cols=block_cols),
        out_shape=jax.ShapeDtypeStruct((peers, members, PAD), BF16),
        in_specs=[pl.BlockSpec(memory_space=pltpu.SMEM)]
        + [pl.BlockSpec(memory_space=pltpu.VMEM)] * 2,
        out_specs=pl.BlockSpec(memory_space=pltpu.VMEM),
        compiler_params=pltpu.CompilerParams(vmem_limit_bytes=16 << 20),
        name="select",
    )(first.reshape(1), perturbations, index)


def swapped(value, bits, count):
    return lax.ppermute(value, "col", [(i, i ^ bits) for i in range(count)])


def gather_col(own, count):
    pair = jnp.concatenate([own, swapped(own, 8, count)])
    half = jnp.concatenate([pair] + [swapped(pair, bits, count) for bits in (2, 6, 4)])
    return half, swapped(half, 1, count)


PIECES = [p ^ q ^ r for r in (0, 1) for q in (0, 2, 6, 4) for p in (0, 8)]


def on_device(perturbations, obs_index, obs_var):
    members_here, group_cols = perturbations.shape
    mem_count = lax.axis_size("mem")
    col_count = lax.axis_size("col")
    members = members_here * mem_count
    block_cols = group_cols // mem_count
    batches = obs_index.shape[0]
    owned = batches * mem_count
    first = lax.axis_index("col").astype(jnp.int32) * group_cols
    sent = select(perturbations, obs_index, first, block_cols, mem_count)
    seen_group = lax.all_to_all(sent, "mem", split_axis=0, concat_axis=0, tiled=True)
    arranged = perturbations.reshape(members_here, mem_count, block_cols).transpose(1, 0, 2)
    arranged, seen_group = lax.optimization_barrier((arranged, seen_group))
    block = lax.all_to_all(arranged, "mem", split_axis=0, concat_axis=0, tiled=True)
    block = block.reshape(members, block_cols)
    seen_group = seen_group.reshape(members, PAD)[:, :owned].T
    near, far = gather_col(seen_group[None], col_count)
    away = (obs_index // group_cols) ^ lax.axis_index("col").astype(jnp.int32)
    piece = sum(jnp.where(away == p, at, 0) for at, p in enumerate(PIECES))
    place = piece * mem_count + obs_index % group_cols // block_cols
    weights = transforms(near, far, place, obs_var, members)
    ensemble = apply(weights, block)
    returned = lax.all_to_all(
        ensemble.reshape(mem_count, members_here, block_cols), "mem",
        split_axis=0, concat_axis=0, tiled=True,
    )
    return returned.transpose(1, 0, 2).reshape(members_here, group_cols)


def solution(mesh):
    return jax.shard_map(
        on_device,
        mesh=mesh,
        in_specs=(P("mem", "col"), P(), P()),
        out_specs=P("mem", "col"),
        check_vma=False,
    )
```

```python
import math

import jax
import jax.numpy as jnp
from jax import lax
from jax.experimental import pallas as pl
from jax.experimental.pallas import tpu as pltpu
from jax.sharding import PartitionSpec as P

F32 = jnp.float32
BF16 = jnp.bfloat16
START = 0.86
STRETCH = (1.07, 1.003)
RESIDUAL_MAX = 3e-2
B_WEIGHT = 300.0
PAD = 128


def mul(a, b):
    return lax.dot_general(
        a.astype(BF16), b.astype(BF16), (((1,), (0,)), ((), ())), preferred_element_type=F32
    )


def mul_t(a, b):
    return lax.dot_general(
        a.astype(BF16), b.astype(BF16), (((1,), (1,)), ((), ())), preferred_element_type=F32
    )


def iotas(n):
    rows = lax.broadcasted_iota(jnp.int32, (n, n), 0)
    cols = lax.broadcasted_iota(jnp.int32, (n, n), 1)
    return rows, cols


def fast_transform(obs, obs_t, var_row, var_col, lower_ref, upper_ref, inverse_count):
    n = obs.shape[1]
    rows, cols = iotas(n)
    wide = obs.astype(F32)
    wide_t = obs_t.astype(F32)
    dr = lax.rsqrt(jnp.sum(wide * wide, axis=0, keepdims=True) * inverse_count + var_row)
    dc = lax.rsqrt(jnp.sum(wide_t * wide_t, axis=1, keepdims=True) * inverse_count + var_col)
    gram = mul_t(obs_t, obs_t)
    error = jnp.where(rows == cols, START - 1.0, gram * (dc * (START * inverse_count)) * dr)
    size = math.sqrt(START * math.prod(STRETCH))
    first_t = wide * (dr * (size * math.sqrt(inverse_count)))
    factor = None
    for step in range(len(STRETCH) + 1):
        near = error.astype(BF16)
        f = near * lower_ref[...]
        if step == 0:
            factor = jnp.where(rows == cols, size, 0.0) - size * f.astype(F32)
        else:
            factor = factor - mul(f, factor)
        first_t = first_t - mul_t(first_t, f)
        if step < len(STRETCH):
            w = mul(f, near)
            y = near * upper_ref[...] - w.astype(BF16)
            error = (error - near.astype(F32)) - (w + mul_t(y, f))
            stretch = STRETCH[step]
            error = error * stretch + jnp.where(rows == cols, stretch - 1.0, 0.0)
    left = jnp.sum(error * error, axis=0, keepdims=True)
    x = jnp.sqrt(var_row) * dr
    diagonal = jnp.sum(jnp.where(rows == cols, factor, 0.0), axis=0, keepdims=True) * x
    scale = 1.0 / (1.0 + diagonal)
    b = jnp.where(rows > cols, factor * (x * scale), 0.0).astype(BF16)
    b2 = mul(b, b).astype(BF16)
    second_t = first_t * scale
    second_t = second_t - mul(second_t, b)
    second_t = second_t + mul(second_t, b2)
    b4 = mul(b2, b2)
    left = left + B_WEIGHT * jnp.sum(b4 * b4, axis=0, keepdims=True)
    second_t = second_t.astype(BF16)
    first_t = first_t.astype(BF16)
    one = jnp.where(rows == cols, 1.0, 0.0)
    turned = (one - mul_t(second_t, first_t)).astype(BF16)
    transform = (one - mul_t(first_t, second_t)).astype(BF16)
    return transform, turned, left


def exact(a, b, dims):
    return lax.dot_general(
        a, b, (dims, ((), ())), precision=lax.Precision.HIGHEST, preferred_element_type=F32
    )


def slow_transform(obs, obs_t, var_row, cov_ref, inv_ref, shift_ref, inverse_count):
    n = obs.shape[1]
    rows, cols = iotas(n)
    on_diagonal = rows == cols
    gram = mul_t(obs_t, obs_t) * inverse_count
    cov_ref[...] = gram + jnp.where(on_diagonal, var_row, 0.0)
    inv_ref[...] = jnp.where(on_diagonal, 1.0, 0.0)
    shift_ref[...] = jnp.where(on_diagonal, 1.0, 0.0)
    lane = lax.broadcasted_iota(jnp.int32, (1, n), 1)
    sublane = lax.broadcasted_iota(jnp.int32, (n, 1), 0)

    def eliminate(j, carry):
        cov = cov_ref[...]
        cov_row = cov_ref[pl.ds(j, 1), :]
        column = jnp.sum(jnp.where(cols == j, cov, 0.0), axis=1, keepdims=True)
        pivot = jnp.sum(jnp.where(lane == j, cov_row, 0.0), axis=1, keepdims=True)
        noise = jnp.sum(jnp.where(lane == j, var_row, 0.0), axis=1, keepdims=True)
        root = jnp.sqrt(pivot)
        below = jnp.where(sublane > j, column / root, 0.0)
        inv_row = inv_ref[pl.ds(j, 1), :] / root
        shift_row = shift_ref[pl.ds(j, 1), :] / (root + jnp.sqrt(noise))
        cov_ref[...] = cov - below * (cov_row / root)
        inv_ref[...] = jnp.where(sublane == j, inv_row, inv_ref[...] - below * inv_row)
        shift_ref[...] = jnp.where(sublane == j, shift_row, shift_ref[...] - below * shift_row)
        return carry

    lax.fori_loop(0, n, eliminate, 0)
    first_t = exact(obs.astype(F32), inv_ref[...], ((1,), (1,)))
    second_t = exact(first_t, shift_ref[...], ((1,), (0,)))
    product = exact(obs.astype(F32), second_t, ((1,), (1,)))
    transform = jnp.where(on_diagonal, 1.0, 0.0) - product * inverse_count
    return transform.astype(BF16)


def transform_kernel(
    near_ref, far_ref, place_ref, var_ref, var_col_ref, weights_ref,
    obs_ref, obs_t_ref, lower_ref, upper_ref, cov_ref, inv_ref, shift_ref, *, inverse_count
):
    batches, observations = var_ref.shape
    pieces, rows_held, members = near_ref.shape
    per_batch = rows_held // batches
    half = pieces * per_batch
    rows, cols = iotas(observations)
    eye = jnp.where(rows == cols, 1.0, 0.0).astype(BF16)

    def load():
        for batch in range(batches):
            order = jnp.where(cols == place_ref[:, batch : batch + 1], 1.0, 0.0)
            held = slice(batch * per_batch, (batch + 1) * per_batch)
            near = near_ref[:, held, :].reshape(half, members)
            far = far_ref[:, held, :].reshape(half, members)
            obs_t = mul(order, jnp.concatenate([near, far])).astype(BF16)
            obs_t_ref[batch] = obs_t
            obs_ref[batch] = mul_t(eye, obs_t).astype(BF16)

    def advance(weights, turned, batch):
        weights_ref[batch] = weights
        for later in range(batch + 1, batches):
            obs_t_ref[later] = mul(obs_t_ref[later], turned).astype(BF16)
            obs_ref[later] = mul(weights, obs_ref[later]).astype(BF16)

    load()
    lower_ref[...] = jnp.where(rows > cols, 1.0, jnp.where(rows == cols, 0.5, 0.0)).astype(BF16)
    upper_ref[...] = jnp.where(rows < cols, 1.0, jnp.where(rows == cols, 0.5, 0.0)).astype(BF16)
    left = jnp.zeros((1, observations), F32)
    for batch in range(batches):
        weights, turned, part = fast_transform(
            obs_ref[batch], obs_t_ref[batch], var_ref[batch : batch + 1, :],
            var_col_ref[:, batch : batch + 1], lower_ref, upper_ref, inverse_count,
        )
        left = left + part
        advance(weights, turned, batch)

    @pl.when(jnp.logical_not(jnp.sum(left) <= RESIDUAL_MAX))
    def _():
        load()
        for batch in range(batches):
            weights = slow_transform(
                obs_ref[batch], obs_t_ref[batch], var_ref[batch : batch + 1, :],
                cov_ref, inv_ref, shift_ref, inverse_count,
            )
            advance(weights, mul_t(eye, weights).astype(BF16), batch)


def transforms(near, far, place, var, var_col, members):
    batches, observations = var.shape
    square = (observations, observations)
    return pl.pallas_call(
        lambda *refs: transform_kernel(
            *refs, inverse_count=1.0 / (members - 1)
        ),
        out_shape=jax.ShapeDtypeStruct((batches, members, members), BF16),
        in_specs=[pl.BlockSpec(memory_space=pltpu.VMEM)] * 5,
        out_specs=pl.BlockSpec(memory_space=pltpu.VMEM),
        scratch_shapes=[
            pltpu.VMEM((batches, members, observations), BF16),
            pltpu.VMEM((batches, observations, members), BF16),
            pltpu.VMEM(square, BF16),
            pltpu.VMEM(square, BF16),
            pltpu.VMEM(square, F32),
            pltpu.VMEM(square, F32),
            pltpu.VMEM(square, F32),
        ],
        compiler_params=pltpu.CompilerParams(vmem_limit_bytes=32 << 20),
        cost_estimate=pl.CostEstimate(flops=1 << 20, bytes_accessed=1 << 10, transcendentals=0),
        name="transforms",
    )(near, far, place, var, var_col)


def apply_kernel(weights_ref, block_ref, out_ref):
    batches = weights_ref.shape[0]
    columns = out_ref.shape[1]
    chunk = min(columns, 512)
    for start in range(0, columns, chunk):
        piece = slice(start, start + chunk)
        part = block_ref[:, piece]
        for batch in range(batches):
            part = mul(weights_ref[batch], part).astype(BF16)
        out_ref[:, piece] = part


def apply(weights, block):
    return pl.pallas_call(
        apply_kernel,
        out_shape=jax.ShapeDtypeStruct(block.shape, BF16),
        in_specs=[pl.BlockSpec(memory_space=pltpu.VMEM)] * 2,
        out_specs=pl.BlockSpec(memory_space=pltpu.VMEM),
        compiler_params=pltpu.CompilerParams(vmem_limit_bytes=16 << 20),
        name="apply",
    )(weights, block)


def select_kernel(
    first_ref, block_ref, index_ref, seen_ref, held_ref, places_ref, sems, *, block_cols
):
    batches = index_ref.shape[0]
    members, group_cols = block_ref.shape
    blocks = group_cols // block_cols
    ranges = [slice(k * block_cols, (k + 1) * block_cols) for k in range(blocks)]
    copies = [pltpu.make_async_copy(index_ref, places_ref, sems.at[blocks])]
    for block, part in enumerate(ranges):
        copies.append(
            pltpu.make_async_copy(block_ref.at[:, part], held_ref.at[:, part], sems.at[block])
        )
    for copy in copies:
        copy.start()
    copies[0].wait()
    local = places_ref[...] - first_ref[0]
    lane = lax.broadcasted_iota(jnp.int32, (1, block_cols), 1)
    slot = lax.broadcasted_iota(jnp.int32, (1, PAD), 1)
    seen = jnp.zeros((members, PAD), F32)
    for block, part in enumerate(ranges):
        inside = local - block * block_cols
        inside = jnp.where((inside >= 0) & (inside < block_cols), inside, 0).astype(F32)
        offsets = jnp.sum(inside, axis=1, keepdims=True).astype(jnp.int32)
        copies[block + 1].wait()
        values = held_ref[:, part].astype(F32)
        for batch in range(batches):
            chosen = jnp.where(lane == offsets[batch : batch + 1, :], values, 0.0)
            column = jnp.sum(chosen, axis=1, keepdims=True)
            seen = jnp.where(slot == batch * blocks + block, column, seen)
    seen = seen.astype(BF16)
    for peer in range(seen_ref.shape[0]):
        seen_ref[peer] = seen


def select(perturbations, index, first, block_cols, peers):
    members, group_cols = perturbations.shape
    return pl.pallas_call(
        lambda *refs: select_kernel(*refs, block_cols=block_cols),
        out_shape=jax.ShapeDtypeStruct((peers, members, PAD), BF16),
        in_specs=[pl.BlockSpec(memory_space=pltpu.SMEM)]
        + [pl.BlockSpec(memory_space=pltpu.HBM)] * 2,
        out_specs=pl.BlockSpec(memory_space=pltpu.VMEM),
        scratch_shapes=[
            pltpu.VMEM(perturbations.shape, BF16),
            pltpu.VMEM(index.shape, jnp.int32),
            pltpu.SemaphoreType.DMA((group_cols // block_cols + 1,)),
        ],
        compiler_params=pltpu.CompilerParams(vmem_limit_bytes=60 << 20),
        name="select",
    )(first.reshape(1), perturbations, index)


def swapped(value, bits, count):
    return lax.ppermute(value, "col", [(i, i ^ bits) for i in range(count)])


def gather_col(own, count):
    pair = jnp.concatenate([own, swapped(own, 8, count)])
    half = jnp.concatenate([pair] + [swapped(pair, bits, count) for bits in (2, 6, 4)])
    return half, swapped(half, 1, count)


PIECES = [p ^ q ^ r for r in (0, 1) for q in (0, 2, 6, 4) for p in (0, 8)]


def on_device(perturbations, obs_index, obs_var):
    members_here, group_cols = perturbations.shape
    mem_count = lax.axis_size("mem")
    col_count = lax.axis_size("col")
    members = members_here * mem_count
    block_cols = group_cols // mem_count
    batches = obs_index.shape[0]
    owned = batches * mem_count
    first = lax.axis_index("col").astype(jnp.int32) * group_cols
    sent = select(perturbations, obs_index, first, block_cols, mem_count)
    seen_group = lax.all_to_all(sent, "mem", split_axis=0, concat_axis=0, tiled=True)
    arranged = perturbations.reshape(members_here, mem_count, block_cols).transpose(1, 0, 2)
    away = (obs_index // group_cols) ^ lax.axis_index("col").astype(jnp.int32)
    piece = sum(jnp.where(away == p, at, 0) for at, p in enumerate(PIECES))
    place = (piece * mem_count + obs_index % group_cols // block_cols).T
    arranged, seen_group, place, var_row, var_col = lax.optimization_barrier(
        (arranged, seen_group, place, obs_var, obs_var.T)
    )
    block = lax.all_to_all(arranged, "mem", split_axis=0, concat_axis=0, tiled=True)
    block = block.reshape(members, block_cols)
    seen_group = seen_group.reshape(members, PAD)[:, :owned].T
    near, far = gather_col(seen_group[None], col_count)
    weights = transforms(near, far, place, var_row, var_col, members)
    ensemble = apply(weights, block)
    returned = lax.all_to_all(
        ensemble.reshape(mem_count, members_here, block_cols), "mem",
        split_axis=0, concat_axis=0, tiled=True,
    )
    return returned.transpose(1, 0, 2).reshape(members_here, group_cols)


def solution(mesh):
    return jax.shard_map(
        on_device,
        mesh=mesh,
        in_specs=(P("mem", "col"), P(), P()),
        out_specs=P("mem", "col"),
        check_vma=False,
    )
```

```python
import math

import jax
import jax.numpy as jnp
from jax import lax
from jax.experimental import pallas as pl
from jax.experimental.pallas import tpu as pltpu
from jax.sharding import PartitionSpec as P

F32 = jnp.float32
BF16 = jnp.bfloat16
START = 0.86
STRETCH = (1.07, 1.003)
RESIDUAL_MAX = 3e-2
B_WEIGHT = 300.0
PAD = 128


def mul(a, b):
    return lax.dot_general(
        a.astype(BF16), b.astype(BF16), (((1,), (0,)), ((), ())), preferred_element_type=F32
    )


def mul_t(a, b):
    return lax.dot_general(
        a.astype(BF16), b.astype(BF16), (((1,), (1,)), ((), ())), preferred_element_type=F32
    )


def iotas(n):
    rows = lax.broadcasted_iota(jnp.int32, (n, n), 0)
    cols = lax.broadcasted_iota(jnp.int32, (n, n), 1)
    return rows, cols


def fast_transform(obs, obs_t, var_row, var_col, lower_ref, upper_ref, inverse_count):
    n = obs.shape[1]
    rows, cols = iotas(n)
    wide = obs.astype(F32)
    wide_t = obs_t.astype(F32)
    dr = lax.rsqrt(jnp.sum(wide * wide, axis=0, keepdims=True) * inverse_count + var_row)
    dc = lax.rsqrt(jnp.sum(wide_t * wide_t, axis=1, keepdims=True) * inverse_count + var_col)
    gram = mul_t(obs_t, obs_t)
    error = jnp.where(rows == cols, START - 1.0, gram * (dc * (START * inverse_count)) * dr)
    size = math.sqrt(START * math.prod(STRETCH))
    first_t = wide * (dr * (size * math.sqrt(inverse_count)))
    factor = None
    for step in range(len(STRETCH) + 1):
        near = error.astype(BF16)
        f = near * lower_ref[...]
        if step == 0:
            factor = jnp.where(rows == cols, size, 0.0) - size * f.astype(F32)
        else:
            factor = factor - mul(f, factor)
        first_t = first_t - mul_t(first_t, f)
        if step < len(STRETCH):
            w = mul(f, near)
            y = near * upper_ref[...] - w.astype(BF16)
            error = (error - near.astype(F32)) - (w + mul_t(y, f))
            stretch = STRETCH[step]
            error = error * stretch + jnp.where(rows == cols, stretch - 1.0, 0.0)
    left = jnp.sum(error * error, axis=0, keepdims=True)
    x = jnp.sqrt(var_row) * dr
    diagonal = jnp.sum(jnp.where(rows == cols, factor, 0.0), axis=0, keepdims=True) * x
    scale = 1.0 / (1.0 + diagonal)
    b = jnp.where(rows > cols, factor * (x * scale), 0.0).astype(BF16)
    b2 = mul(b, b).astype(BF16)
    second_t = first_t * scale
    second_t = second_t - mul(second_t, b)
    second_t = second_t + mul(second_t, b2)
    b4 = mul(b2, b2)
    left = left + B_WEIGHT * jnp.sum(b4 * b4, axis=0, keepdims=True)
    second_t = second_t.astype(BF16)
    first_t = first_t.astype(BF16)
    one = jnp.where(rows == cols, 1.0, 0.0)
    turned = (one - mul_t(second_t, first_t)).astype(BF16)
    transform = (one - mul_t(first_t, second_t)).astype(BF16)
    return transform, turned, left


def exact(a, b, dims):
    return lax.dot_general(
        a, b, (dims, ((), ())), precision=lax.Precision.HIGHEST, preferred_element_type=F32
    )


def slow_transform(obs, obs_t, var_row, cov_ref, inv_ref, shift_ref, inverse_count):
    n = obs.shape[1]
    rows, cols = iotas(n)
    on_diagonal = rows == cols
    gram = mul_t(obs_t, obs_t) * inverse_count
    cov_ref[...] = gram + jnp.where(on_diagonal, var_row, 0.0)
    inv_ref[...] = jnp.where(on_diagonal, 1.0, 0.0)
    shift_ref[...] = jnp.where(on_diagonal, 1.0, 0.0)
    lane = lax.broadcasted_iota(jnp.int32, (1, n), 1)
    sublane = lax.broadcasted_iota(jnp.int32, (n, 1), 0)

    def eliminate(j, carry):
        cov = cov_ref[...]
        cov_row = cov_ref[pl.ds(j, 1), :]
        column = jnp.sum(jnp.where(cols == j, cov, 0.0), axis=1, keepdims=True)
        pivot = jnp.sum(jnp.where(lane == j, cov_row, 0.0), axis=1, keepdims=True)
        noise = jnp.sum(jnp.where(lane == j, var_row, 0.0), axis=1, keepdims=True)
        root = jnp.sqrt(pivot)
        below = jnp.where(sublane > j, column / root, 0.0)
        inv_row = inv_ref[pl.ds(j, 1), :] / root
        shift_row = shift_ref[pl.ds(j, 1), :] / (root + jnp.sqrt(noise))
        cov_ref[...] = cov - below * (cov_row / root)
        inv_ref[...] = jnp.where(sublane == j, inv_row, inv_ref[...] - below * inv_row)
        shift_ref[...] = jnp.where(sublane == j, shift_row, shift_ref[...] - below * shift_row)
        return carry

    lax.fori_loop(0, n, eliminate, 0)
    first_t = exact(obs.astype(F32), inv_ref[...], ((1,), (1,)))
    second_t = exact(first_t, shift_ref[...], ((1,), (0,)))
    product = exact(obs.astype(F32), second_t, ((1,), (1,)))
    transform = jnp.where(on_diagonal, 1.0, 0.0) - product * inverse_count
    return transform.astype(BF16)


def transform_kernel(
    near_ref, far_ref, place_ref, var_ref, var_col_ref, weights_ref,
    obs_ref, obs_t_ref, lower_ref, upper_ref, cov_ref, inv_ref, shift_ref, *, inverse_count
):
    batches, observations = var_ref.shape
    pieces, rows_held, members = near_ref.shape
    per_batch = rows_held // batches
    half = pieces * per_batch
    rows, cols = iotas(observations)
    eye = jnp.where(rows == cols, 1.0, 0.0).astype(BF16)

    def load():
        for batch in range(batches):
            order = jnp.where(cols == place_ref[:, batch : batch + 1], 1.0, 0.0)
            held = slice(batch * per_batch, (batch + 1) * per_batch)
            near = near_ref[:, held, :].reshape(half, members)
            far = far_ref[:, held, :].reshape(half, members)
            obs_t = mul(order, jnp.concatenate([near, far])).astype(BF16)
            obs_t_ref[batch] = obs_t
            obs_ref[batch] = mul_t(eye, obs_t).astype(BF16)

    def advance(weights, turned, batch):
        weights_ref[batch] = weights
        for later in range(batch + 1, batches):
            obs_t_ref[later] = mul(obs_t_ref[later], turned).astype(BF16)
            obs_ref[later] = mul(weights, obs_ref[later]).astype(BF16)

    load()
    lower_ref[...] = jnp.where(rows > cols, 1.0, jnp.where(rows == cols, 0.5, 0.0)).astype(BF16)
    upper_ref[...] = jnp.where(rows < cols, 1.0, jnp.where(rows == cols, 0.5, 0.0)).astype(BF16)
    left = jnp.zeros((1, observations), F32)
    for batch in range(batches):
        weights, turned, part = fast_transform(
            obs_ref[batch], obs_t_ref[batch], var_ref[batch : batch + 1, :],
            var_col_ref[:, batch : batch + 1], lower_ref, upper_ref, inverse_count,
        )
        left = left + part
        advance(weights, turned, batch)

    @pl.when(jnp.logical_not(jnp.sum(left) <= RESIDUAL_MAX))
    def _():
        load()
        for batch in range(batches):
            weights = slow_transform(
                obs_ref[batch], obs_t_ref[batch], var_ref[batch : batch + 1, :],
                cov_ref, inv_ref, shift_ref, inverse_count,
            )
            advance(weights, mul_t(eye, weights).astype(BF16), batch)


def transforms(near, far, place, var, var_col, members):
    batches, observations = var.shape
    square = (observations, observations)
    return pl.pallas_call(
        lambda *refs: transform_kernel(
            *refs, inverse_count=1.0 / (members - 1)
        ),
        out_shape=jax.ShapeDtypeStruct((batches, members, members), BF16),
        in_specs=[pl.BlockSpec(memory_space=pltpu.VMEM)] * 5,
        out_specs=pl.BlockSpec(memory_space=pltpu.VMEM),
        scratch_shapes=[
            pltpu.VMEM((batches, members, observations), BF16),
            pltpu.VMEM((batches, observations, members), BF16),
            pltpu.VMEM(square, BF16),
            pltpu.VMEM(square, BF16),
            pltpu.VMEM(square, F32),
            pltpu.VMEM(square, F32),
            pltpu.VMEM(square, F32),
        ],
        compiler_params=pltpu.CompilerParams(vmem_limit_bytes=32 << 20),
        cost_estimate=pl.CostEstimate(flops=3 * 10**9, bytes_accessed=1 << 10, transcendentals=0),
        name="transforms",
    )(near, far, place, var, var_col)


def apply_kernel(weights_ref, block_ref, out_ref):
    batches = weights_ref.shape[0]
    columns = out_ref.shape[1]
    chunk = min(columns, 512)
    for start in range(0, columns, chunk):
        piece = slice(start, start + chunk)
        part = block_ref[:, piece]
        for batch in range(batches):
            part = mul(weights_ref[batch], part).astype(BF16)
        out_ref[:, piece] = part


def apply(weights, block):
    return pl.pallas_call(
        apply_kernel,
        out_shape=jax.ShapeDtypeStruct(block.shape, BF16),
        in_specs=[pl.BlockSpec(memory_space=pltpu.VMEM)] * 2,
        out_specs=pl.BlockSpec(memory_space=pltpu.VMEM),
        compiler_params=pltpu.CompilerParams(vmem_limit_bytes=16 << 20),
        name="apply",
    )(weights, block)


def select_kernel(
    first_ref, block_ref, index_ref, seen_ref, held_ref, places_ref, sems, *, block_cols
):
    batches = index_ref.shape[0]
    members, group_cols = block_ref.shape
    blocks = group_cols // block_cols
    ranges = [slice(k * block_cols, (k + 1) * block_cols) for k in range(blocks)]
    fetch_places = pltpu.make_async_copy(index_ref, places_ref, sems.at[0])
    fetch_block = pltpu.make_async_copy(block_ref, held_ref, sems.at[1])
    fetch_places.start()
    fetch_block.start()
    fetch_places.wait()
    local = places_ref[...] - first_ref[0]
    lane = lax.broadcasted_iota(jnp.int32, (1, block_cols), 1)
    slot = lax.broadcasted_iota(jnp.int32, (1, PAD), 1)
    offsets = []
    for block in range(blocks):
        inside = local - block * block_cols
        inside = jnp.where((inside >= 0) & (inside < block_cols), inside, 0).astype(F32)
        offsets.append(jnp.sum(inside, axis=1, keepdims=True).astype(jnp.int32))
    fetch_block.wait()
    seen = jnp.zeros((members, PAD), F32)
    for block, part in enumerate(ranges):
        values = held_ref[:, part].astype(F32)
        for batch in range(batches):
            chosen = jnp.where(lane == offsets[block][batch : batch + 1, :], values, 0.0)
            column = jnp.sum(chosen, axis=1, keepdims=True)
            seen = jnp.where(slot == batch * blocks + block, column, seen)
    seen = seen.astype(BF16)
    for peer in range(seen_ref.shape[0]):
        seen_ref[peer] = seen


def select(perturbations, index, first, block_cols, peers):
    members = perturbations.shape[0]
    return pl.pallas_call(
        lambda *refs: select_kernel(*refs, block_cols=block_cols),
        out_shape=jax.ShapeDtypeStruct((peers, members, PAD), BF16),
        in_specs=[pl.BlockSpec(memory_space=pltpu.SMEM)]
        + [pl.BlockSpec(memory_space=pltpu.HBM)] * 2,
        out_specs=pl.BlockSpec(memory_space=pltpu.VMEM),
        scratch_shapes=[
            pltpu.VMEM(perturbations.shape, BF16),
            pltpu.VMEM(index.shape, jnp.int32),
            pltpu.SemaphoreType.DMA((2,)),
        ],
        compiler_params=pltpu.CompilerParams(vmem_limit_bytes=60 << 20),
        name="select",
    )(first.reshape(1), perturbations, index)


def swapped(value, bits, count):
    return lax.ppermute(value, "col", [(i, i ^ bits) for i in range(count)])


def gather_col(own, count):
    pair = jnp.concatenate([own, swapped(own, 8, count)])
    half = jnp.concatenate([pair] + [swapped(pair, bits, count) for bits in (2, 6, 4)])
    return half, swapped(half, 1, count)


PIECES = [p ^ q ^ r for r in (0, 1) for q in (0, 2, 6, 4) for p in (0, 8)]


def on_device(perturbations, obs_index, obs_var):
    members_here, group_cols = perturbations.shape
    mem_count = lax.axis_size("mem")
    col_count = lax.axis_size("col")
    members = members_here * mem_count
    block_cols = group_cols // mem_count
    batches = obs_index.shape[0]
    owned = batches * mem_count
    first = lax.axis_index("col").astype(jnp.int32) * group_cols
    sent = select(perturbations, obs_index, first, block_cols, mem_count)
    seen_group = lax.all_to_all(sent, "mem", split_axis=0, concat_axis=0, tiled=True)
    arranged = perturbations.reshape(members_here, mem_count, block_cols).transpose(1, 0, 2)
    away = (obs_index // group_cols) ^ lax.axis_index("col").astype(jnp.int32)
    piece = sum(jnp.where(away == p, at, 0) for at, p in enumerate(PIECES))
    place = (piece * mem_count + obs_index % group_cols // block_cols).T
    arranged, seen_group, place, var_row, var_col = lax.optimization_barrier(
        (arranged, seen_group, place, obs_var, obs_var.T)
    )
    block = lax.all_to_all(arranged, "mem", split_axis=0, concat_axis=0, tiled=True)
    block = block.reshape(members, block_cols)
    seen_group = seen_group.reshape(members, PAD)[:, :owned].T
    near, far = gather_col(seen_group[None], col_count)
    weights = transforms(near, far, place, var_row, var_col, members)
    ensemble = apply(weights, block)
    returned = lax.all_to_all(
        ensemble.reshape(mem_count, members_here, block_cols), "mem",
        split_axis=0, concat_axis=0, tiled=True,
    )
    return returned.transpose(1, 0, 2).reshape(members_here, group_cols)


def solution(mesh):
    return jax.shard_map(
        on_device,
        mesh=mesh,
        in_specs=(P("mem", "col"), P(), P()),
        out_specs=P("mem", "col"),
        check_vma=False,
    )
```

```python
import math

import jax
import jax.numpy as jnp
from jax import lax
from jax.experimental import pallas as pl
from jax.experimental.pallas import tpu as pltpu
from jax.sharding import PartitionSpec as P

F32 = jnp.float32
BF16 = jnp.bfloat16
START = 0.86
STRETCH = (1.07, 1.003)
RESIDUAL_MAX = 3e-2
B_WEIGHT = 300.0
PAD = 128


def mul(a, b):
    return lax.dot_general(
        a.astype(BF16), b.astype(BF16), (((1,), (0,)), ((), ())), preferred_element_type=F32
    )


def mul_t(a, b):
    return lax.dot_general(
        a.astype(BF16), b.astype(BF16), (((1,), (1,)), ((), ())), preferred_element_type=F32
    )


def iotas(n):
    rows = lax.broadcasted_iota(jnp.int32, (n, n), 0)
    cols = lax.broadcasted_iota(jnp.int32, (n, n), 1)
    return rows, cols


def fast_transform(obs, obs_t, var_row, var_col, lower_ref, upper_ref, inverse_count):
    n = obs.shape[1]
    rows, cols = iotas(n)
    wide = obs.astype(F32)
    wide_t = obs_t.astype(F32)
    dr = lax.rsqrt(jnp.sum(wide * wide, axis=0, keepdims=True) * inverse_count + var_row)
    dc = lax.rsqrt(jnp.sum(wide_t * wide_t, axis=1, keepdims=True) * inverse_count + var_col)
    gram = mul_t(obs_t, obs_t)
    error = jnp.where(rows == cols, START - 1.0, gram * (dc * (START * inverse_count)) * dr)
    size = math.sqrt(START * math.prod(STRETCH))
    first_t = wide * (dr * (size * math.sqrt(inverse_count)))
    factor = None
    for step in range(len(STRETCH) + 1):
        near = error.astype(BF16)
        f = near * lower_ref[...]
        if step == 0:
            factor = jnp.where(rows == cols, size, 0.0) - size * f.astype(F32)
        else:
            factor = factor - mul(f, factor)
        first_t = first_t - mul_t(first_t, f)
        if step < len(STRETCH):
            w = mul(f, near)
            y = near * upper_ref[...] - w.astype(BF16)
            error = (error - near.astype(F32)) - (w + mul_t(y, f))
            stretch = STRETCH[step]
            error = error * stretch + jnp.where(rows == cols, stretch - 1.0, 0.0)
    left = jnp.sum(error * error, axis=0, keepdims=True)
    x = jnp.sqrt(var_row) * dr
    diagonal = jnp.sum(jnp.where(rows == cols, factor, 0.0), axis=0, keepdims=True) * x
    scale = 1.0 / (1.0 + diagonal)
    b = jnp.where(rows > cols, factor * (x * scale), 0.0).astype(BF16)
    b2 = mul(b, b).astype(BF16)
    second_t = first_t * scale
    second_t = second_t - mul(second_t, b)
    second_t = second_t + mul(second_t, b2)
    b4 = mul(b2, b2)
    left = left + B_WEIGHT * jnp.sum(b4 * b4, axis=0, keepdims=True)
    second_t = second_t.astype(BF16)
    first_t = first_t.astype(BF16)
    one = jnp.where(rows == cols, 1.0, 0.0)
    turned = (one - mul_t(second_t, first_t)).astype(BF16)
    transform = (one - mul_t(first_t, second_t)).astype(BF16)
    return transform, turned, left


def exact(a, b, dims):
    return lax.dot_general(
        a, b, (dims, ((), ())), precision=lax.Precision.HIGHEST, preferred_element_type=F32
    )


def slow_transform(obs, obs_t, var_row, cov_ref, inv_ref, shift_ref, inverse_count):
    n = obs.shape[1]
    rows, cols = iotas(n)
    on_diagonal = rows == cols
    gram = mul_t(obs_t, obs_t) * inverse_count
    cov_ref[...] = gram + jnp.where(on_diagonal, var_row, 0.0)
    inv_ref[...] = jnp.where(on_diagonal, 1.0, 0.0)
    shift_ref[...] = jnp.where(on_diagonal, 1.0, 0.0)
    lane = lax.broadcasted_iota(jnp.int32, (1, n), 1)
    sublane = lax.broadcasted_iota(jnp.int32, (n, 1), 0)

    def eliminate(j, carry):
        cov = cov_ref[...]
        cov_row = cov_ref[pl.ds(j, 1), :]
        column = jnp.sum(jnp.where(cols == j, cov, 0.0), axis=1, keepdims=True)
        pivot = jnp.sum(jnp.where(lane == j, cov_row, 0.0), axis=1, keepdims=True)
        noise = jnp.sum(jnp.where(lane == j, var_row, 0.0), axis=1, keepdims=True)
        root = jnp.sqrt(pivot)
        below = jnp.where(sublane > j, column / root, 0.0)
        inv_row = inv_ref[pl.ds(j, 1), :] / root
        shift_row = shift_ref[pl.ds(j, 1), :] / (root + jnp.sqrt(noise))
        cov_ref[...] = cov - below * (cov_row / root)
        inv_ref[...] = jnp.where(sublane == j, inv_row, inv_ref[...] - below * inv_row)
        shift_ref[...] = jnp.where(sublane == j, shift_row, shift_ref[...] - below * shift_row)
        return carry

    lax.fori_loop(0, n, eliminate, 0)
    first_t = exact(obs.astype(F32), inv_ref[...], ((1,), (1,)))
    second_t = exact(first_t, shift_ref[...], ((1,), (0,)))
    product = exact(obs.astype(F32), second_t, ((1,), (1,)))
    transform = jnp.where(on_diagonal, 1.0, 0.0) - product * inverse_count
    return transform.astype(BF16)


def transform_kernel(
    *refs, inverse_count
):
    (*part_refs, place_ref, var_ref, var_col_ref, weights_ref,
     obs_ref, obs_t_ref, lower_ref, upper_ref, cov_ref, inv_ref, shift_ref) = refs
    batches, observations = var_ref.shape
    pieces, rows_held, members = part_refs[0].shape
    per_batch = rows_held // batches
    rows, cols = iotas(observations)
    eye = jnp.where(rows == cols, 1.0, 0.0).astype(BF16)

    def load():
        for batch in range(batches):
            order = jnp.where(cols == place_ref[:, batch : batch + 1], 1.0, 0.0)
            held = slice(batch * per_batch, (batch + 1) * per_batch)
            parts = [ref[:, held, :].reshape(pieces * per_batch, members) for ref in part_refs]
            obs_t = mul(order, jnp.concatenate(parts)).astype(BF16)
            obs_t_ref[batch] = obs_t
            obs_ref[batch] = mul_t(eye, obs_t).astype(BF16)

    def advance(weights, turned, batch):
        weights_ref[batch] = weights
        for later in range(batch + 1, batches):
            obs_t_ref[later] = mul(obs_t_ref[later], turned).astype(BF16)
            obs_ref[later] = mul(weights, obs_ref[later]).astype(BF16)

    load()
    lower_ref[...] = jnp.where(rows > cols, 1.0, jnp.where(rows == cols, 0.5, 0.0)).astype(BF16)
    upper_ref[...] = jnp.where(rows < cols, 1.0, jnp.where(rows == cols, 0.5, 0.0)).astype(BF16)
    left = jnp.zeros((1, observations), F32)
    for batch in range(batches):
        weights, turned, part = fast_transform(
            obs_ref[batch], obs_t_ref[batch], var_ref[batch : batch + 1, :],
            var_col_ref[:, batch : batch + 1], lower_ref, upper_ref, inverse_count,
        )
        left = left + part
        advance(weights, turned, batch)

    @pl.when(jnp.logical_not(jnp.sum(left) <= RESIDUAL_MAX))
    def _():
        load()
        for batch in range(batches):
            weights = slow_transform(
                obs_ref[batch], obs_t_ref[batch], var_ref[batch : batch + 1, :],
                cov_ref, inv_ref, shift_ref, inverse_count,
            )
            advance(weights, mul_t(eye, weights).astype(BF16), batch)


def transforms(parts, place, var, var_col, members):
    batches, observations = var.shape
    square = (observations, observations)
    return pl.pallas_call(
        lambda *refs: transform_kernel(
            *refs, inverse_count=1.0 / (members - 1)
        ),
        out_shape=jax.ShapeDtypeStruct((batches, members, members), BF16),
        in_specs=[pl.BlockSpec(memory_space=pltpu.VMEM)] * (len(parts) + 3),
        out_specs=pl.BlockSpec(memory_space=pltpu.VMEM),
        scratch_shapes=[
            pltpu.VMEM((batches, members, observations), BF16),
            pltpu.VMEM((batches, observations, members), BF16),
            pltpu.VMEM(square, BF16),
            pltpu.VMEM(square, BF16),
            pltpu.VMEM(square, F32),
            pltpu.VMEM(square, F32),
            pltpu.VMEM(square, F32),
        ],
        compiler_params=pltpu.CompilerParams(vmem_limit_bytes=32 << 20),
        cost_estimate=pl.CostEstimate(flops=8 * 10**9, bytes_accessed=1 << 10, transcendentals=0),
        name="transforms",
    )(*parts, place, var, var_col)


def apply_kernel(weights_ref, block_ref, out_ref):
    batches = weights_ref.shape[0]
    columns = out_ref.shape[1]
    chunk = min(columns, 512)
    for start in range(0, columns, chunk):
        piece = slice(start, start + chunk)
        part = block_ref[:, piece]
        for batch in range(batches):
            part = mul(weights_ref[batch], part).astype(BF16)
        out_ref[:, piece] = part


def apply(weights, block):
    return pl.pallas_call(
        apply_kernel,
        out_shape=jax.ShapeDtypeStruct(block.shape, BF16),
        in_specs=[pl.BlockSpec(memory_space=pltpu.VMEM)] * 2,
        out_specs=pl.BlockSpec(memory_space=pltpu.VMEM),
        compiler_params=pltpu.CompilerParams(vmem_limit_bytes=16 << 20),
        name="apply",
    )(weights, block)


def select_kernel(
    first_ref, block_ref, index_ref, seen_ref, held_ref, places_ref, sems, *, block_cols
):
    batches = index_ref.shape[0]
    members, group_cols = block_ref.shape
    blocks = group_cols // block_cols
    ranges = [slice(k * block_cols, (k + 1) * block_cols) for k in range(blocks)]
    fetch_places = pltpu.make_async_copy(index_ref, places_ref, sems.at[0])
    fetch_block = pltpu.make_async_copy(block_ref, held_ref, sems.at[1])
    fetch_places.start()
    fetch_block.start()
    fetch_places.wait()
    local = places_ref[...] - first_ref[0]
    lane = lax.broadcasted_iota(jnp.int32, (1, block_cols), 1)
    slot = lax.broadcasted_iota(jnp.int32, (1, PAD), 1)
    offsets = []
    for block in range(blocks):
        inside = local - block * block_cols
        inside = jnp.where((inside >= 0) & (inside < block_cols), inside, 0).astype(F32)
        offsets.append(jnp.sum(inside, axis=1, keepdims=True).astype(jnp.int32))
    fetch_block.wait()
    seen = jnp.zeros((members, PAD), F32)
    for block, part in enumerate(ranges):
        values = held_ref[:, part].astype(F32)
        for batch in range(batches):
            chosen = jnp.where(lane == offsets[block][batch : batch + 1, :], values, 0.0)
            column = jnp.sum(chosen, axis=1, keepdims=True)
            seen = jnp.where(slot == batch * blocks + block, column, seen)
    seen = seen.astype(BF16)
    for peer in range(seen_ref.shape[0]):
        seen_ref[peer] = seen


def select(perturbations, index, first, block_cols, peers):
    members = perturbations.shape[0]
    return pl.pallas_call(
        lambda *refs: select_kernel(*refs, block_cols=block_cols),
        out_shape=jax.ShapeDtypeStruct((peers, members, PAD), BF16),
        in_specs=[pl.BlockSpec(memory_space=pltpu.SMEM)]
        + [pl.BlockSpec(memory_space=pltpu.HBM)] * 2,
        out_specs=pl.BlockSpec(memory_space=pltpu.VMEM),
        scratch_shapes=[
            pltpu.VMEM(perturbations.shape, BF16),
            pltpu.VMEM(index.shape, jnp.int32),
            pltpu.SemaphoreType.DMA((2,)),
        ],
        compiler_params=pltpu.CompilerParams(vmem_limit_bytes=60 << 20),
        name="select",
    )(first.reshape(1), perturbations, index)


def swapped(value, bits, count):
    return lax.ppermute(value, "col", [(i, i ^ bits) for i in range(count)])


def gather_col(own, count):
    pair = jnp.concatenate([own, swapped(own, 8, count)])
    return [pair] + [swapped(pair, bits, count) for bits in (2, 6, 4)]


PIECES = [q ^ p for q in (0, 2, 6, 4) for p in (0, 8)]
CORES = 2


def chip_groups(mem_count, col_count):
    return [
        [mem * col_count + first + core for core in range(CORES) for mem in range(mem_count)]
        for first in range(0, col_count, CORES)
    ]


def on_device(perturbations, obs_index, obs_var):
    members_here, group_cols = perturbations.shape
    mem_count = lax.axis_size("mem")
    col_count = lax.axis_size("col")
    members = members_here * mem_count
    block_cols = group_cols // mem_count
    batches = obs_index.shape[0]
    owned = batches * mem_count
    first = lax.axis_index("col").astype(jnp.int32) * group_cols
    sent = select(perturbations, obs_index, first, block_cols, CORES * mem_count)
    seen_group = lax.all_to_all(
        sent, ("mem", "col"), split_axis=0, concat_axis=0, tiled=True,
        axis_index_groups=chip_groups(mem_count, col_count),
    )
    arranged = perturbations.reshape(members_here, mem_count, block_cols).transpose(1, 0, 2)
    owner = obs_index // group_cols
    away = (owner ^ lax.axis_index("col").astype(jnp.int32)) // CORES * CORES
    piece = sum(jnp.where(away == p, at * CORES, 0) for at, p in enumerate(PIECES)) + owner % CORES
    place = (piece * mem_count + obs_index % group_cols // block_cols).T
    arranged, seen_group, place, var_row, var_col = lax.optimization_barrier(
        (arranged, seen_group, place, obs_var, obs_var.T)
    )
    block = lax.all_to_all(arranged, "mem", split_axis=0, concat_axis=0, tiled=True)
    block = block.reshape(members, block_cols)
    seen_group = seen_group.reshape(CORES, members, PAD)[:, :, :owned].transpose(0, 2, 1)
    parts = gather_col(seen_group, col_count)
    weights = transforms(parts, place, var_row, var_col, members)
    ensemble = apply(weights, block)
    returned = lax.all_to_all(
        ensemble.reshape(mem_count, members_here, block_cols), "mem",
        split_axis=0, concat_axis=0, tiled=True,
    )
    return returned.transpose(1, 0, 2).reshape(members_here, group_cols)


def solution(mesh):
    return jax.shard_map(
        on_device,
        mesh=mesh,
        in_specs=(P("mem", "col"), P(), P()),
        out_specs=P("mem", "col"),
        check_vma=False,
    )
```

```python
import math

import jax
import jax.numpy as jnp
from jax import lax
from jax.experimental import pallas as pl
from jax.experimental.pallas import tpu as pltpu
from jax.sharding import PartitionSpec as P

F32 = jnp.float32
BF16 = jnp.bfloat16
START = 0.86
STRETCH = (1.07, 1.003)
RESIDUAL_MAX = 3e-2
B_WEIGHT = 300.0
PAD = 128


def mul(a, b):
    return lax.dot_general(
        a.astype(BF16), b.astype(BF16), (((1,), (0,)), ((), ())), preferred_element_type=F32
    )


def mul_t(a, b):
    return lax.dot_general(
        a.astype(BF16), b.astype(BF16), (((1,), (1,)), ((), ())), preferred_element_type=F32
    )


def iotas(n):
    rows = lax.broadcasted_iota(jnp.int32, (n, n), 0)
    cols = lax.broadcasted_iota(jnp.int32, (n, n), 1)
    return rows, cols


def fast_transform(obs, obs_t, var_row, var_col, lower_ref, upper_ref, inverse_count):
    n = obs.shape[1]
    rows, cols = iotas(n)
    wide = obs.astype(F32)
    wide_t = obs_t.astype(F32)
    dr = lax.rsqrt(jnp.sum(wide * wide, axis=0, keepdims=True) * inverse_count + var_row)
    dc = lax.rsqrt(jnp.sum(wide_t * wide_t, axis=1, keepdims=True) * inverse_count + var_col)
    gram = mul_t(obs_t, obs_t)
    error = jnp.where(rows == cols, START - 1.0, gram * (dc * (START * inverse_count)) * dr)
    size = math.sqrt(START * math.prod(STRETCH))
    first_t = wide * (dr * (size * math.sqrt(inverse_count)))
    factor = None
    for step in range(len(STRETCH) + 1):
        near = error.astype(BF16)
        f = near * lower_ref[...]
        if step == 0:
            factor = jnp.where(rows == cols, size, 0.0) - size * f.astype(F32)
        else:
            factor = factor - mul(f, factor)
        first_t = first_t - mul_t(first_t, f)
        if step < len(STRETCH):
            w = mul(f, near)
            y = near * upper_ref[...] - w.astype(BF16)
            error = (error - near.astype(F32)) - (w + mul_t(y, f))
            stretch = STRETCH[step]
            error = error * stretch + jnp.where(rows == cols, stretch - 1.0, 0.0)
    left = jnp.sum(error * error, axis=0, keepdims=True)
    x = jnp.sqrt(var_row) * dr
    diagonal = jnp.sum(jnp.where(rows == cols, factor, 0.0), axis=0, keepdims=True) * x
    scale = 1.0 / (1.0 + diagonal)
    b = jnp.where(rows > cols, factor * (x * scale), 0.0).astype(BF16)
    b2 = mul(b, b).astype(BF16)
    second_t = first_t * scale
    second_t = second_t - mul(second_t, b)
    second_t = second_t + mul(second_t, b2)
    b4 = mul(b2, b2)
    left = left + B_WEIGHT * jnp.sum(b4 * b4, axis=0, keepdims=True)
    second_t = second_t.astype(BF16)
    first_t = first_t.astype(BF16)
    one = jnp.where(rows == cols, 1.0, 0.0)
    turned = (one - mul_t(second_t, first_t)).astype(BF16)
    transform = (one - mul_t(first_t, second_t)).astype(BF16)
    return transform, turned, left


def exact(a, b, dims):
    return lax.dot_general(
        a, b, (dims, ((), ())), precision=lax.Precision.HIGHEST, preferred_element_type=F32
    )


def slow_transform(obs, obs_t, var_row, cov_ref, inv_ref, shift_ref, inverse_count):
    n = obs.shape[1]
    rows, cols = iotas(n)
    on_diagonal = rows == cols
    gram = mul_t(obs_t, obs_t) * inverse_count
    cov_ref[...] = gram + jnp.where(on_diagonal, var_row, 0.0)
    inv_ref[...] = jnp.where(on_diagonal, 1.0, 0.0)
    shift_ref[...] = jnp.where(on_diagonal, 1.0, 0.0)
    lane = lax.broadcasted_iota(jnp.int32, (1, n), 1)
    sublane = lax.broadcasted_iota(jnp.int32, (n, 1), 0)

    def eliminate(j, carry):
        cov = cov_ref[...]
        cov_row = cov_ref[pl.ds(j, 1), :]
        column = jnp.sum(jnp.where(cols == j, cov, 0.0), axis=1, keepdims=True)
        pivot = jnp.sum(jnp.where(lane == j, cov_row, 0.0), axis=1, keepdims=True)
        noise = jnp.sum(jnp.where(lane == j, var_row, 0.0), axis=1, keepdims=True)
        root = jnp.sqrt(pivot)
        below = jnp.where(sublane > j, column / root, 0.0)
        inv_row = inv_ref[pl.ds(j, 1), :] / root
        shift_row = shift_ref[pl.ds(j, 1), :] / (root + jnp.sqrt(noise))
        cov_ref[...] = cov - below * (cov_row / root)
        inv_ref[...] = jnp.where(sublane == j, inv_row, inv_ref[...] - below * inv_row)
        shift_ref[...] = jnp.where(sublane == j, shift_row, shift_ref[...] - below * shift_row)
        return carry

    lax.fori_loop(0, n, eliminate, 0)
    first_t = exact(obs.astype(F32), inv_ref[...], ((1,), (1,)))
    second_t = exact(first_t, shift_ref[...], ((1,), (0,)))
    product = exact(obs.astype(F32), second_t, ((1,), (1,)))
    transform = jnp.where(on_diagonal, 1.0, 0.0) - product * inverse_count
    return transform.astype(BF16)


def transform_kernel(
    *refs, inverse_count
):
    (*part_refs, place_ref, var_ref, var_col_ref, weights_ref,
     obs_ref, obs_t_ref, lower_ref, upper_ref, cov_ref, inv_ref, shift_ref) = refs
    batches, observations = var_ref.shape
    pieces, rows_held, members = part_refs[0].shape
    per_batch = rows_held // batches
    rows, cols = iotas(observations)
    eye = jnp.where(rows == cols, 1.0, 0.0).astype(BF16)

    def load():
        for batch in range(batches):
            order = jnp.where(cols == place_ref[:, batch : batch + 1], 1.0, 0.0)
            held = slice(batch * per_batch, (batch + 1) * per_batch)
            parts = [ref[:, held, :].reshape(pieces * per_batch, members) for ref in part_refs]
            obs_t = mul(order, jnp.concatenate(parts)).astype(BF16)
            obs_t_ref[batch] = obs_t
            obs_ref[batch] = mul_t(eye, obs_t).astype(BF16)

    def advance(weights, turned, batch):
        weights_ref[batch] = weights
        for later in range(batch + 1, batches):
            obs_t_ref[later] = mul(obs_t_ref[later], turned).astype(BF16)
            obs_ref[later] = mul(weights, obs_ref[later]).astype(BF16)

    load()
    lower_ref[...] = jnp.where(rows > cols, 1.0, jnp.where(rows == cols, 0.5, 0.0)).astype(BF16)
    upper_ref[...] = jnp.where(rows < cols, 1.0, jnp.where(rows == cols, 0.5, 0.0)).astype(BF16)
    left = jnp.zeros((1, observations), F32)
    for batch in range(batches):
        weights, turned, part = fast_transform(
            obs_ref[batch], obs_t_ref[batch], var_ref[batch : batch + 1, :],
            var_col_ref[:, batch : batch + 1], lower_ref, upper_ref, inverse_count,
        )
        left = left + part
        advance(weights, turned, batch)

    @pl.when(jnp.logical_not(jnp.sum(left) <= RESIDUAL_MAX))
    def _():
        load()
        for batch in range(batches):
            weights = slow_transform(
                obs_ref[batch], obs_t_ref[batch], var_ref[batch : batch + 1, :],
                cov_ref, inv_ref, shift_ref, inverse_count,
            )
            advance(weights, mul_t(eye, weights).astype(BF16), batch)


def transforms(parts, place, var, var_col, members):
    batches, observations = var.shape
    square = (observations, observations)
    return pl.pallas_call(
        lambda *refs: transform_kernel(
            *refs, inverse_count=1.0 / (members - 1)
        ),
        out_shape=jax.ShapeDtypeStruct((batches, members, members), BF16),
        in_specs=[pl.BlockSpec(memory_space=pltpu.VMEM)] * (len(parts) + 3),
        out_specs=pl.BlockSpec(memory_space=pltpu.VMEM),
        scratch_shapes=[
            pltpu.VMEM((batches, members, observations), BF16),
            pltpu.VMEM((batches, observations, members), BF16),
            pltpu.VMEM(square, BF16),
            pltpu.VMEM(square, BF16),
            pltpu.VMEM(square, F32),
            pltpu.VMEM(square, F32),
            pltpu.VMEM(square, F32),
        ],
        compiler_params=pltpu.CompilerParams(vmem_limit_bytes=32 << 20),
        cost_estimate=pl.CostEstimate(flops=8 * 10**9, bytes_accessed=1 << 10, transcendentals=0),
        name="transforms",
    )(*parts, place, var, var_col)


def apply_kernel(weights_ref, block_ref, out_ref):
    batches = weights_ref.shape[0]
    columns = out_ref.shape[1]
    chunk = min(columns, 1024)
    for start in range(0, columns, chunk):
        piece = slice(start, start + chunk)
        part = block_ref[:, piece]
        for batch in range(batches):
            part = mul(weights_ref[batch], part).astype(BF16)
        out_ref[:, piece] = part


def apply(weights, block):
    return pl.pallas_call(
        apply_kernel,
        out_shape=jax.ShapeDtypeStruct(block.shape, BF16),
        in_specs=[pl.BlockSpec(memory_space=pltpu.VMEM)] * 2,
        out_specs=pl.BlockSpec(memory_space=pltpu.VMEM),
        compiler_params=pltpu.CompilerParams(vmem_limit_bytes=16 << 20),
        name="apply",
    )(weights, block)


def select_kernel(
    first_ref, block_ref, index_ref, seen_ref, held_ref, places_ref, sems, *, block_cols
):
    batches = index_ref.shape[0]
    members, group_cols = block_ref.shape
    blocks = group_cols // block_cols
    ranges = [slice(k * block_cols, (k + 1) * block_cols) for k in range(blocks)]
    fetch_places = pltpu.make_async_copy(index_ref, places_ref, sems.at[0])
    fetch_block = pltpu.make_async_copy(block_ref, held_ref, sems.at[1])
    fetch_places.start()
    fetch_block.start()
    fetch_places.wait()
    local = places_ref[...] - first_ref[0]
    lane = lax.broadcasted_iota(jnp.int32, (1, block_cols), 1)
    slot = lax.broadcasted_iota(jnp.int32, (1, PAD), 1)
    offsets = []
    for block in range(blocks):
        inside = local - block * block_cols
        inside = jnp.where((inside >= 0) & (inside < block_cols), inside, 0).astype(F32)
        offsets.append(jnp.sum(inside, axis=1, keepdims=True).astype(jnp.int32))
    fetch_block.wait()
    seen = jnp.zeros((members, PAD), F32)
    for block, part in enumerate(ranges):
        values = held_ref[:, part].astype(F32)
        for batch in range(batches):
            chosen = jnp.where(lane == offsets[block][batch : batch + 1, :], values, 0.0)
            column = jnp.sum(chosen, axis=1, keepdims=True)
            seen = jnp.where(slot == batch * blocks + block, column, seen)
    seen = seen.astype(BF16)
    for peer in range(seen_ref.shape[0]):
        seen_ref[peer] = seen


def select(perturbations, index, first, block_cols, peers):
    members = perturbations.shape[0]
    return pl.pallas_call(
        lambda *refs: select_kernel(*refs, block_cols=block_cols),
        out_shape=jax.ShapeDtypeStruct((peers, members, PAD), BF16),
        in_specs=[pl.BlockSpec(memory_space=pltpu.SMEM)]
        + [pl.BlockSpec(memory_space=pltpu.HBM)] * 2,
        out_specs=pl.BlockSpec(memory_space=pltpu.VMEM),
        scratch_shapes=[
            pltpu.VMEM(perturbations.shape, BF16),
            pltpu.VMEM(index.shape, jnp.int32),
            pltpu.SemaphoreType.DMA((2,)),
        ],
        compiler_params=pltpu.CompilerParams(vmem_limit_bytes=60 << 20),
        name="select",
    )(first.reshape(1), perturbations, index)


def swapped(value, bits, count):
    return lax.ppermute(value, "col", [(i, i ^ bits) for i in range(count)])


def gather_col(own, count):
    pair = jnp.concatenate([own, swapped(own, 8, count)])
    return [pair] + [swapped(pair, bits, count) for bits in (2, 6, 4)]


PIECES = [q ^ p for q in (0, 2, 6, 4) for p in (0, 8)]
CORES = 2


def chip_groups(mem_count, col_count):
    return [
        [mem * col_count + first + core for core in range(CORES) for mem in range(mem_count)]
        for first in range(0, col_count, CORES)
    ]


def on_device(perturbations, obs_index, obs_var):
    members_here, group_cols = perturbations.shape
    mem_count = lax.axis_size("mem")
    col_count = lax.axis_size("col")
    members = members_here * mem_count
    block_cols = group_cols // mem_count
    batches = obs_index.shape[0]
    owned = batches * mem_count
    first = lax.axis_index("col").astype(jnp.int32) * group_cols
    sent = select(perturbations, obs_index, first, block_cols, CORES * mem_count)
    seen_group = lax.all_to_all(
        sent, ("mem", "col"), split_axis=0, concat_axis=0, tiled=True,
        axis_index_groups=chip_groups(mem_count, col_count),
    )
    arranged = perturbations.reshape(members_here, mem_count, block_cols).transpose(1, 0, 2)
    owner = obs_index // group_cols
    away = (owner ^ lax.axis_index("col").astype(jnp.int32)) // CORES * CORES
    piece = sum(jnp.where(away == p, at * CORES, 0) for at, p in enumerate(PIECES)) + owner % CORES
    place = (piece * mem_count + obs_index % group_cols // block_cols).T
    arranged, seen_group, place, var_row, var_col = lax.optimization_barrier(
        (arranged, seen_group, place, obs_var, obs_var.T)
    )
    block = lax.all_to_all(arranged, "mem", split_axis=0, concat_axis=0, tiled=True)
    block = block.reshape(members, block_cols)
    seen_group = seen_group.reshape(CORES, members, PAD)[:, :, :owned].transpose(0, 2, 1)
    parts = gather_col(seen_group, col_count)
    weights = transforms(parts, place, var_row, var_col, members)
    ensemble = apply(weights, block)
    returned = lax.all_to_all(
        ensemble.reshape(mem_count, members_here, block_cols), "mem",
        split_axis=0, concat_axis=0, tiled=True,
    )
    return returned.transpose(1, 0, 2).reshape(members_here, group_cols)


def solution(mesh):
    return jax.shard_map(
        on_device,
        mesh=mesh,
        in_specs=(P("mem", "col"), P(), P()),
        out_specs=P("mem", "col"),
        check_vma=False,
    )
```

```python
import math

import jax
import jax.numpy as jnp
from jax import lax
from jax.experimental import pallas as pl
from jax.experimental.pallas import tpu as pltpu
from jax.sharding import PartitionSpec as P

F32 = jnp.float32
BF16 = jnp.bfloat16
START = 0.86
STRETCH = (1.07, 1.003)
RESIDUAL_MAX = 3e-2
B_WEIGHT = 300.0
PAD = 128


def mul(a, b):
    return lax.dot_general(
        a.astype(BF16), b.astype(BF16), (((1,), (0,)), ((), ())), preferred_element_type=F32
    )


def mul_t(a, b):
    return lax.dot_general(
        a.astype(BF16), b.astype(BF16), (((1,), (1,)), ((), ())), preferred_element_type=F32
    )


def iotas(n):
    rows = lax.broadcasted_iota(jnp.int32, (n, n), 0)
    cols = lax.broadcasted_iota(jnp.int32, (n, n), 1)
    return rows, cols


def fast_transform(obs, obs_t, var_row, var_col, lower_ref, upper_ref, inverse_count):
    n = obs.shape[1]
    rows, cols = iotas(n)
    wide = obs.astype(F32)
    wide_t = obs_t.astype(F32)
    dr = lax.rsqrt(jnp.sum(wide * wide, axis=0, keepdims=True) * inverse_count + var_row)
    dc = lax.rsqrt(jnp.sum(wide_t * wide_t, axis=1, keepdims=True) * inverse_count + var_col)
    gram = mul_t(obs_t, obs_t)
    error = jnp.where(rows == cols, START - 1.0, gram * (dc * (START * inverse_count)) * dr)
    size = math.sqrt(START * math.prod(STRETCH))
    first_t = wide * (dr * (size * math.sqrt(inverse_count)))
    factor = None
    for step in range(len(STRETCH) + 1):
        near = error.astype(BF16)
        f = near * lower_ref[...]
        if step == 0:
            factor = jnp.where(rows == cols, size, 0.0) - size * f.astype(F32)
        else:
            factor = factor - mul(f, factor)
        first_t = first_t - mul_t(first_t, f)
        if step < len(STRETCH):
            w = mul(f, near)
            y = near * upper_ref[...] - w.astype(BF16)
            error = (error - near.astype(F32)) - (w + mul_t(y, f))
            stretch = STRETCH[step]
            error = error * stretch + jnp.where(rows == cols, stretch - 1.0, 0.0)
    left = jnp.sum(error * error, axis=0, keepdims=True)
    x = jnp.sqrt(var_row) * dr
    diagonal = jnp.sum(jnp.where(rows == cols, factor, 0.0), axis=0, keepdims=True) * x
    scale = 1.0 / (1.0 + diagonal)
    b = jnp.where(rows > cols, factor * (x * scale), 0.0).astype(BF16)
    b2 = mul(b, b).astype(BF16)
    second_t = first_t * scale
    second_t = second_t - mul(second_t, b)
    second_t = second_t + mul(second_t, b2)
    b4 = mul(b2, b2)
    left = left + B_WEIGHT * jnp.sum(b4 * b4, axis=0, keepdims=True)
    second_t = second_t.astype(BF16)
    first_t = first_t.astype(BF16)
    one = jnp.where(rows == cols, 1.0, 0.0)
    turned = (one - mul_t(second_t, first_t)).astype(BF16)
    transform = (one - mul_t(first_t, second_t)).astype(BF16)
    return transform, turned, left


def exact(a, b, dims):
    return lax.dot_general(
        a, b, (dims, ((), ())), precision=lax.Precision.HIGHEST, preferred_element_type=F32
    )


def slow_transform(obs, obs_t, var_row, cov_ref, inv_ref, shift_ref, inverse_count):
    n = obs.shape[1]
    rows, cols = iotas(n)
    on_diagonal = rows == cols
    gram = mul_t(obs_t, obs_t) * inverse_count
    cov_ref[...] = gram + jnp.where(on_diagonal, var_row, 0.0)
    inv_ref[...] = jnp.where(on_diagonal, 1.0, 0.0)
    shift_ref[...] = jnp.where(on_diagonal, 1.0, 0.0)
    lane = lax.broadcasted_iota(jnp.int32, (1, n), 1)
    sublane = lax.broadcasted_iota(jnp.int32, (n, 1), 0)

    def eliminate(j, carry):
        cov = cov_ref[...]
        cov_row = cov_ref[pl.ds(j, 1), :]
        column = jnp.sum(jnp.where(cols == j, cov, 0.0), axis=1, keepdims=True)
        pivot = jnp.sum(jnp.where(lane == j, cov_row, 0.0), axis=1, keepdims=True)
        noise = jnp.sum(jnp.where(lane == j, var_row, 0.0), axis=1, keepdims=True)
        root = jnp.sqrt(pivot)
        below = jnp.where(sublane > j, column / root, 0.0)
        inv_row = inv_ref[pl.ds(j, 1), :] / root
        shift_row = shift_ref[pl.ds(j, 1), :] / (root + jnp.sqrt(noise))
        cov_ref[...] = cov - below * (cov_row / root)
        inv_ref[...] = jnp.where(sublane == j, inv_row, inv_ref[...] - below * inv_row)
        shift_ref[...] = jnp.where(sublane == j, shift_row, shift_ref[...] - below * shift_row)
        return carry

    lax.fori_loop(0, n, eliminate, 0)
    first_t = exact(obs.astype(F32), inv_ref[...], ((1,), (1,)))
    second_t = exact(first_t, shift_ref[...], ((1,), (0,)))
    product = exact(obs.astype(F32), second_t, ((1,), (1,)))
    transform = jnp.where(on_diagonal, 1.0, 0.0) - product * inverse_count
    return transform.astype(BF16)


def transform_kernel(
    *refs, inverse_count
):
    (*part_refs, place_ref, var_ref, var_col_ref, weights_ref,
     obs_ref, obs_t_ref, lower_ref, upper_ref, cov_ref, inv_ref, shift_ref) = refs
    batches, observations = var_ref.shape
    _, rows_held, members = part_refs[0].shape
    per_batch = rows_held // batches
    rows, cols = iotas(observations)
    eye = jnp.where(rows == cols, 1.0, 0.0).astype(BF16)

    def load():
        for batch in range(batches):
            order = jnp.where(cols == place_ref[:, batch : batch + 1], 1.0, 0.0)
            held = slice(batch * per_batch, (batch + 1) * per_batch)
            parts = [
                ref[:, held, :].reshape(ref.shape[0] * per_batch, members) for ref in part_refs
            ]
            obs_t = mul(order, jnp.concatenate(parts)).astype(BF16)
            obs_t_ref[batch] = obs_t
            obs_ref[batch] = mul_t(eye, obs_t).astype(BF16)

    def advance(weights, turned, batch):
        weights_ref[batch] = weights
        for later in range(batch + 1, batches):
            obs_t_ref[later] = mul(obs_t_ref[later], turned).astype(BF16)
            obs_ref[later] = mul(weights, obs_ref[later]).astype(BF16)

    load()
    lower_ref[...] = jnp.where(rows > cols, 1.0, jnp.where(rows == cols, 0.5, 0.0)).astype(BF16)
    upper_ref[...] = jnp.where(rows < cols, 1.0, jnp.where(rows == cols, 0.5, 0.0)).astype(BF16)
    left = jnp.zeros((1, observations), F32)
    for batch in range(batches):
        weights, turned, part = fast_transform(
            obs_ref[batch], obs_t_ref[batch], var_ref[batch : batch + 1, :],
            var_col_ref[:, batch : batch + 1], lower_ref, upper_ref, inverse_count,
        )
        left = left + part
        advance(weights, turned, batch)

    @pl.when(jnp.logical_not(jnp.sum(left) <= RESIDUAL_MAX))
    def _():
        load()
        for batch in range(batches):
            weights = slow_transform(
                obs_ref[batch], obs_t_ref[batch], var_ref[batch : batch + 1, :],
                cov_ref, inv_ref, shift_ref, inverse_count,
            )
            advance(weights, mul_t(eye, weights).astype(BF16), batch)


def transforms(parts, place, var, var_col, members):
    batches, observations = var.shape
    square = (observations, observations)
    return pl.pallas_call(
        lambda *refs: transform_kernel(
            *refs, inverse_count=1.0 / (members - 1)
        ),
        out_shape=jax.ShapeDtypeStruct((batches, members, members), BF16),
        in_specs=[pl.BlockSpec(memory_space=pltpu.VMEM)] * (len(parts) + 3),
        out_specs=pl.BlockSpec(memory_space=pltpu.VMEM),
        scratch_shapes=[
            pltpu.VMEM((batches, members, observations), BF16),
            pltpu.VMEM((batches, observations, members), BF16),
            pltpu.VMEM(square, BF16),
            pltpu.VMEM(square, BF16),
            pltpu.VMEM(square, F32),
            pltpu.VMEM(square, F32),
            pltpu.VMEM(square, F32),
        ],
        compiler_params=pltpu.CompilerParams(vmem_limit_bytes=32 << 20),
        cost_estimate=pl.CostEstimate(flops=8 * 10**9, bytes_accessed=1 << 10, transcendentals=0),
        name="transforms",
    )(*parts, place, var, var_col)


def apply_kernel(weights_ref, block_ref, out_ref):
    batches = weights_ref.shape[0]
    columns = out_ref.shape[1]
    chunk = min(columns, 1024)
    for start in range(0, columns, chunk):
        piece = slice(start, start + chunk)
        part = block_ref[:, piece]
        for batch in range(batches):
            part = mul(weights_ref[batch], part).astype(BF16)
        out_ref[:, piece] = part


def apply(weights, block):
    return pl.pallas_call(
        apply_kernel,
        out_shape=jax.ShapeDtypeStruct(block.shape, BF16),
        in_specs=[pl.BlockSpec(memory_space=pltpu.VMEM)] * 2,
        out_specs=pl.BlockSpec(memory_space=pltpu.VMEM),
        compiler_params=pltpu.CompilerParams(vmem_limit_bytes=16 << 20),
        name="apply",
    )(weights, block)


def select_kernel(
    first_ref, block_ref, index_ref, seen_ref, held_ref, places_ref, sems, *, block_cols
):
    batches = index_ref.shape[0]
    members, group_cols = block_ref.shape
    blocks = group_cols // block_cols
    ranges = [slice(k * block_cols, (k + 1) * block_cols) for k in range(blocks)]
    fetch_places = pltpu.make_async_copy(index_ref, places_ref, sems.at[0])
    fetch_block = pltpu.make_async_copy(block_ref, held_ref, sems.at[1])
    fetch_places.start()
    fetch_block.start()
    fetch_places.wait()
    local = places_ref[...] - first_ref[0]
    lane = lax.broadcasted_iota(jnp.int32, (1, block_cols), 1)
    slot = lax.broadcasted_iota(jnp.int32, (1, PAD), 1)
    offsets = []
    for block in range(blocks):
        inside = local - block * block_cols
        inside = jnp.where((inside >= 0) & (inside < block_cols), inside, 0).astype(F32)
        offsets.append(jnp.sum(inside, axis=1, keepdims=True).astype(jnp.int32))
    fetch_block.wait()
    seen = jnp.zeros((members, PAD), F32)
    for block, part in enumerate(ranges):
        values = held_ref[:, part].astype(F32)
        for batch in range(batches):
            chosen = jnp.where(lane == offsets[block][batch : batch + 1, :], values, 0.0)
            column = jnp.sum(chosen, axis=1, keepdims=True)
            seen = jnp.where(slot == batch * blocks + block, column, seen)
    seen = seen.astype(BF16)
    for peer in range(seen_ref.shape[0]):
        seen_ref[peer] = seen


def select(perturbations, index, first, block_cols, peers):
    members = perturbations.shape[0]
    return pl.pallas_call(
        lambda *refs: select_kernel(*refs, block_cols=block_cols),
        out_shape=jax.ShapeDtypeStruct((peers, members, PAD), BF16),
        in_specs=[pl.BlockSpec(memory_space=pltpu.SMEM)]
        + [pl.BlockSpec(memory_space=pltpu.HBM)] * 2,
        out_specs=pl.BlockSpec(memory_space=pltpu.VMEM),
        scratch_shapes=[
            pltpu.VMEM(perturbations.shape, BF16),
            pltpu.VMEM(index.shape, jnp.int32),
            pltpu.SemaphoreType.DMA((2,)),
        ],
        compiler_params=pltpu.CompilerParams(vmem_limit_bytes=60 << 20),
        name="select",
    )(first.reshape(1), perturbations, index)


def swapped(value, bits, count):
    return lax.ppermute(value, "col", [(i, i ^ bits) for i in range(count)])


def gather_col(own, count):
    across = swapped(own, 4, count)
    pair = jnp.concatenate([own, swapped(own, 8, count)])
    return [pair, swapped(pair, 2, count), swapped(pair, 6, count), across, swapped(across, 8, count)]


PIECES = [q ^ p for q in (0, 2, 6, 4) for p in (0, 8)]
CORES = 2


def chip_groups(mem_count, col_count):
    return [
        [mem * col_count + first + core for core in range(CORES) for mem in range(mem_count)]
        for first in range(0, col_count, CORES)
    ]


def on_device(perturbations, obs_index, obs_var):
    members_here, group_cols = perturbations.shape
    mem_count = lax.axis_size("mem")
    col_count = lax.axis_size("col")
    members = members_here * mem_count
    block_cols = group_cols // mem_count
    batches = obs_index.shape[0]
    owned = batches * mem_count
    first = lax.axis_index("col").astype(jnp.int32) * group_cols
    sent = select(perturbations, obs_index, first, block_cols, CORES * mem_count)
    seen_group = lax.all_to_all(
        sent, ("mem", "col"), split_axis=0, concat_axis=0, tiled=True,
        axis_index_groups=chip_groups(mem_count, col_count),
    )
    arranged = perturbations.reshape(members_here, mem_count, block_cols).transpose(1, 0, 2)
    owner = obs_index // group_cols
    away = (owner ^ lax.axis_index("col").astype(jnp.int32)) // CORES * CORES
    piece = sum(jnp.where(away == p, at * CORES, 0) for at, p in enumerate(PIECES)) + owner % CORES
    place = (piece * mem_count + obs_index % group_cols // block_cols).T
    arranged, seen_group, place, var_row, var_col = lax.optimization_barrier(
        (arranged, seen_group, place, obs_var, obs_var.T)
    )
    block = lax.all_to_all(arranged, "mem", split_axis=0, concat_axis=0, tiled=True)
    block = block.reshape(members, block_cols)
    seen_group = seen_group.reshape(CORES, members, PAD)[:, :, :owned].transpose(0, 2, 1)
    parts = gather_col(seen_group, col_count)
    weights = transforms(parts, place, var_row, var_col, members)
    ensemble = apply(weights, block)
    returned = lax.all_to_all(
        ensemble.reshape(mem_count, members_here, block_cols), "mem",
        split_axis=0, concat_axis=0, tiled=True,
    )
    return returned.transpose(1, 0, 2).reshape(members_here, group_cols)


def solution(mesh):
    return jax.shard_map(
        on_device,
        mesh=mesh,
        in_specs=(P("mem", "col"), P(), P()),
        out_specs=P("mem", "col"),
        check_vma=False,
    )
```

```python
import math

import jax
import jax.numpy as jnp
from jax import lax
from jax.experimental import pallas as pl
from jax.experimental.pallas import tpu as pltpu
from jax.sharding import PartitionSpec as P

F32 = jnp.float32
BF16 = jnp.bfloat16
START = 0.86
STRETCH = 1.07
STEPS = 3
RESIDUAL_MAX = 3e-2
B_WEIGHT = 300.0
PAD = 128


def mul(a, b):
    return lax.dot_general(
        a.astype(BF16), b.astype(BF16), (((1,), (0,)), ((), ())), preferred_element_type=F32
    )


def mul_t(a, b):
    return lax.dot_general(
        a.astype(BF16), b.astype(BF16), (((1,), (1,)), ((), ())), preferred_element_type=F32
    )


def iotas(n):
    rows = lax.broadcasted_iota(jnp.int32, (n, n), 0)
    cols = lax.broadcasted_iota(jnp.int32, (n, n), 1)
    return rows, cols


def fast_transform(obs, obs_t, var_row, var_col, eye_ref, lower_ref, upper_ref, inverse_count):
    wide = obs.astype(F32)
    wide_t = obs_t.astype(F32)
    dr = lax.rsqrt(jnp.sum(wide * wide, axis=0, keepdims=True) * inverse_count + var_row)
    dc = lax.rsqrt(jnp.sum(wide_t * wide_t, axis=1, keepdims=True) * inverse_count + var_col)
    rows, cols = iotas(obs.shape[1])
    near = mul_t(obs_t, obs_t) * (dc * (-START * inverse_count)) * dr
    near = jnp.where(rows == cols, 1.0 - START, near).astype(BF16)
    size = math.sqrt(START * STRETCH)
    first_t = wide * (dr * (size * math.sqrt(inverse_count)))
    factor = None
    for step in range(STEPS):
        f = near * lower_ref[...]
        if step == 0:
            factor = (eye_ref[...] - f.astype(F32)) * size
        else:
            factor = factor - mul(f, factor)
        first_t = first_t - mul_t(first_t, f)
        if step < STEPS - 1:
            w = mul(f, near)
            y = near * upper_ref[...] + w.astype(BF16)
            error = mul_t(y, f) - w
            if step == 0:
                error = error * STRETCH - eye_ref[...] * (STRETCH - 1.0)
            near = error.astype(BF16)
    left = jnp.sum(error * error, axis=0, keepdims=True)
    x = jnp.sqrt(var_row) * dr
    diagonal = jnp.sum(eye_ref[...] * factor, axis=0, keepdims=True) * x
    scale = 1.0 / (1.0 + diagonal)
    b = jnp.where(rows > cols, factor * (x * scale), 0.0).astype(BF16)
    b2 = mul(b, b).astype(BF16)
    second_t = first_t * scale
    second_t = second_t - mul(second_t, b)
    second_t = second_t + mul(second_t, b2)
    b4 = mul(b2, b2)
    left = left + B_WEIGHT * jnp.sum(b4 * b4, axis=0, keepdims=True)
    second_t = second_t.astype(BF16)
    first_t = first_t.astype(BF16)
    turned = (eye_ref[...] - mul_t(second_t, first_t)).astype(BF16)
    transform = (eye_ref[...] - mul_t(first_t, second_t)).astype(BF16)
    return transform, turned, left


def exact(a, b, dims):
    return lax.dot_general(
        a, b, (dims, ((), ())), precision=lax.Precision.HIGHEST, preferred_element_type=F32
    )


def slow_transform(obs, obs_t, var_row, cov_ref, inv_ref, shift_ref, inverse_count):
    n = obs.shape[1]
    rows, cols = iotas(n)
    on_diagonal = rows == cols
    gram = mul_t(obs_t, obs_t) * inverse_count
    cov_ref[...] = gram + jnp.where(on_diagonal, var_row, 0.0)
    inv_ref[...] = jnp.where(on_diagonal, 1.0, 0.0)
    shift_ref[...] = jnp.where(on_diagonal, 1.0, 0.0)
    lane = lax.broadcasted_iota(jnp.int32, (1, n), 1)
    sublane = lax.broadcasted_iota(jnp.int32, (n, 1), 0)

    def eliminate(j, carry):
        cov = cov_ref[...]
        cov_row = cov_ref[pl.ds(j, 1), :]
        column = jnp.sum(jnp.where(cols == j, cov, 0.0), axis=1, keepdims=True)
        pivot = jnp.sum(jnp.where(lane == j, cov_row, 0.0), axis=1, keepdims=True)
        noise = jnp.sum(jnp.where(lane == j, var_row, 0.0), axis=1, keepdims=True)
        root = jnp.sqrt(pivot)
        below = jnp.where(sublane > j, column / root, 0.0)
        inv_row = inv_ref[pl.ds(j, 1), :] / root
        shift_row = shift_ref[pl.ds(j, 1), :] / (root + jnp.sqrt(noise))
        cov_ref[...] = cov - below * (cov_row / root)
        inv_ref[...] = jnp.where(sublane == j, inv_row, inv_ref[...] - below * inv_row)
        shift_ref[...] = jnp.where(sublane == j, shift_row, shift_ref[...] - below * shift_row)
        return carry

    lax.fori_loop(0, n, eliminate, 0)
    first_t = exact(obs.astype(F32), inv_ref[...], ((1,), (1,)))
    second_t = exact(first_t, shift_ref[...], ((1,), (0,)))
    product = exact(obs.astype(F32), second_t, ((1,), (1,)))
    transform = jnp.where(on_diagonal, 1.0, 0.0) - product * inverse_count
    return transform.astype(BF16)


def transform_kernel(
    *refs, inverse_count
):
    (*part_refs, place_ref, var_ref, var_col_ref, weights_ref,
     obs_ref, obs_t_ref, eye_ref, lower_ref, upper_ref, cov_ref, inv_ref, shift_ref) = refs
    batches, observations = var_ref.shape
    pieces, rows_held, members = part_refs[0].shape
    per_batch = rows_held // batches
    rows, cols = iotas(observations)
    eye = jnp.where(rows == cols, 1.0, 0.0).astype(BF16)

    def load():
        for batch in range(batches):
            order = jnp.where(cols == place_ref[:, batch : batch + 1], 1.0, 0.0)
            held = slice(batch * per_batch, (batch + 1) * per_batch)
            parts = [ref[:, held, :].reshape(pieces * per_batch, members) for ref in part_refs]
            obs_t = mul(order, jnp.concatenate(parts)).astype(BF16)
            obs_t_ref[batch] = obs_t
            obs_ref[batch] = mul_t(eye, obs_t).astype(BF16)

    def advance(weights, turned, batch):
        weights_ref[batch] = weights
        for later in range(batch + 1, batches):
            obs_t_ref[later] = mul(obs_t_ref[later], turned).astype(BF16)
            obs_ref[later] = mul(weights, obs_ref[later]).astype(BF16)

    load()
    eye_ref[...] = jnp.where(rows == cols, 1.0, 0.0)
    lower_ref[...] = jnp.where(rows > cols, -1.0, jnp.where(rows == cols, -0.5, 0.0)).astype(BF16)
    upper_ref[...] = jnp.where(rows < cols, -1.0, jnp.where(rows == cols, -0.5, 0.0)).astype(BF16)
    left = jnp.zeros((1, observations), F32)
    for batch in range(batches):
        weights, turned, part = fast_transform(
            obs_ref[batch], obs_t_ref[batch], var_ref[batch : batch + 1, :],
            var_col_ref[:, batch : batch + 1], eye_ref, lower_ref, upper_ref, inverse_count,
        )
        left = left + part
        advance(weights, turned, batch)

    @pl.when(jnp.logical_not(jnp.sum(left) <= RESIDUAL_MAX))
    def _():
        load()
        for batch in range(batches):
            weights = slow_transform(
                obs_ref[batch], obs_t_ref[batch], var_ref[batch : batch + 1, :],
                cov_ref, inv_ref, shift_ref, inverse_count,
            )
            advance(weights, mul_t(eye, weights).astype(BF16), batch)


def transforms(parts, place, var, var_col, members):
    batches, observations = var.shape
    square = (observations, observations)
    return pl.pallas_call(
        lambda *refs: transform_kernel(
            *refs, inverse_count=1.0 / (members - 1)
        ),
        out_shape=jax.ShapeDtypeStruct((batches, members, members), BF16),
        in_specs=[pl.BlockSpec(memory_space=pltpu.VMEM)] * (len(parts) + 3),
        out_specs=pl.BlockSpec(memory_space=pltpu.VMEM),
        scratch_shapes=[
            pltpu.VMEM((batches, members, observations), BF16),
            pltpu.VMEM((batches, observations, members), BF16),
            pltpu.VMEM(square, F32),
            pltpu.VMEM(square, BF16),
            pltpu.VMEM(square, BF16),
            pltpu.VMEM(square, F32),
            pltpu.VMEM(square, F32),
            pltpu.VMEM(square, F32),
        ],
        compiler_params=pltpu.CompilerParams(vmem_limit_bytes=32 << 20),
        cost_estimate=pl.CostEstimate(flops=8 * 10**9, bytes_accessed=1 << 10, transcendentals=0),
        name="transforms",
    )(*parts, place, var, var_col)


def apply_kernel(weights_ref, block_ref, out_ref):
    batches = weights_ref.shape[0]
    columns = out_ref.shape[1]
    chunk = min(columns, 1024)
    for start in range(0, columns, chunk):
        piece = slice(start, start + chunk)
        part = block_ref[:, piece]
        for batch in range(batches):
            part = mul(weights_ref[batch], part).astype(BF16)
        out_ref[:, piece] = part


def apply(weights, block):
    return pl.pallas_call(
        apply_kernel,
        out_shape=jax.ShapeDtypeStruct(block.shape, BF16),
        in_specs=[pl.BlockSpec(memory_space=pltpu.VMEM)] * 2,
        out_specs=pl.BlockSpec(memory_space=pltpu.VMEM),
        compiler_params=pltpu.CompilerParams(vmem_limit_bytes=16 << 20),
        name="apply",
    )(weights, block)


def select_kernel(
    first_ref, block_ref, index_ref, seen_ref, held_ref, places_ref, sems, *, block_cols
):
    batches = index_ref.shape[0]
    members, group_cols = block_ref.shape
    blocks = group_cols // block_cols
    ranges = [slice(k * block_cols, (k + 1) * block_cols) for k in range(blocks)]
    fetch_places = pltpu.make_async_copy(index_ref, places_ref, sems.at[0])
    fetch_block = pltpu.make_async_copy(block_ref, held_ref, sems.at[1])
    fetch_places.start()
    fetch_block.start()
    fetch_places.wait()
    local = places_ref[...] - first_ref[0]
    lane = lax.broadcasted_iota(jnp.int32, (1, block_cols), 1)
    slot = lax.broadcasted_iota(jnp.int32, (1, PAD), 1)
    offsets = []
    for block in range(blocks):
        inside = local - block * block_cols
        inside = jnp.where((inside >= 0) & (inside < block_cols), inside, 0).astype(F32)
        offsets.append(jnp.sum(inside, axis=1, keepdims=True).astype(jnp.int32))
    fetch_block.wait()
    seen = jnp.zeros((members, PAD), F32)
    for block, part in enumerate(ranges):
        values = held_ref[:, part].astype(F32)
        for batch in range(batches):
            chosen = jnp.where(lane == offsets[block][batch : batch + 1, :], values, 0.0)
            column = jnp.sum(chosen, axis=1, keepdims=True)
            seen = jnp.where(slot == batch * blocks + block, column, seen)
    seen = seen.astype(BF16)
    for peer in range(seen_ref.shape[0]):
        seen_ref[peer] = seen


def select(perturbations, index, first, block_cols, peers):
    members = perturbations.shape[0]
    return pl.pallas_call(
        lambda *refs: select_kernel(*refs, block_cols=block_cols),
        out_shape=jax.ShapeDtypeStruct((peers, members, PAD), BF16),
        in_specs=[pl.BlockSpec(memory_space=pltpu.SMEM)]
        + [pl.BlockSpec(memory_space=pltpu.HBM)] * 2,
        out_specs=pl.BlockSpec(memory_space=pltpu.VMEM),
        scratch_shapes=[
            pltpu.VMEM(perturbations.shape, BF16),
            pltpu.VMEM(index.shape, jnp.int32),
            pltpu.SemaphoreType.DMA((2,)),
        ],
        compiler_params=pltpu.CompilerParams(vmem_limit_bytes=60 << 20),
        name="select",
    )(first.reshape(1), perturbations, index)


def swapped(value, bits, count):
    return lax.ppermute(value, "col", [(i, i ^ bits) for i in range(count)])


def gather_col(own, count):
    pair = jnp.concatenate([own, swapped(own, 8, count)])
    return [pair] + [swapped(pair, bits, count) for bits in (2, 6, 4)]


PIECES = [q ^ p for q in (0, 2, 6, 4) for p in (0, 8)]
CORES = 2


def chip_groups(mem_count, col_count):
    return [
        [mem * col_count + first + core for core in range(CORES) for mem in range(mem_count)]
        for first in range(0, col_count, CORES)
    ]


def on_device(perturbations, obs_index, obs_var):
    members_here, group_cols = perturbations.shape
    mem_count = lax.axis_size("mem")
    col_count = lax.axis_size("col")
    members = members_here * mem_count
    block_cols = group_cols // mem_count
    batches = obs_index.shape[0]
    owned = batches * mem_count
    first = lax.axis_index("col").astype(jnp.int32) * group_cols
    sent = select(perturbations, obs_index, first, block_cols, CORES * mem_count)
    seen_group = lax.all_to_all(
        sent, ("mem", "col"), split_axis=0, concat_axis=0, tiled=True,
        axis_index_groups=chip_groups(mem_count, col_count),
    )
    arranged = perturbations.reshape(members_here, mem_count, block_cols).transpose(1, 0, 2)
    owner = obs_index // group_cols
    away = (owner ^ lax.axis_index("col").astype(jnp.int32)) // CORES * CORES
    piece = sum(jnp.where(away == p, at * CORES, 0) for at, p in enumerate(PIECES)) + owner % CORES
    place = (piece * mem_count + obs_index % group_cols // block_cols).T
    arranged, seen_group, place, var_row, var_col = lax.optimization_barrier(
        (arranged, seen_group, place, obs_var, obs_var.T)
    )
    block = lax.all_to_all(arranged, "mem", split_axis=0, concat_axis=0, tiled=True)
    block = block.reshape(members, block_cols)
    seen_group = seen_group.reshape(CORES, members, PAD)[:, :, :owned].transpose(0, 2, 1)
    parts = gather_col(seen_group, col_count)
    weights = transforms(parts, place, var_row, var_col, members)
    ensemble = apply(weights, block)
    returned = lax.all_to_all(
        ensemble.reshape(mem_count, members_here, block_cols), "mem",
        split_axis=0, concat_axis=0, tiled=True,
    )
    return returned.transpose(1, 0, 2).reshape(members_here, group_cols)


def solution(mesh):
    return jax.shard_map(
        on_device,
        mesh=mesh,
        in_specs=(P("mem", "col"), P(), P()),
        out_specs=P("mem", "col"),
        check_vma=False,
    )
```
